256 devices in a mesh: seq: 32 (over z, x), head: 8 (over y, core).
Axes of the slice: x: 4, y: 4, z: 8, core: 2. Of those that a mesh axis runs over, the one named last changes fastest.
Arguments:
- layer_input: bfloat16 [4096, 8192], P('seq'), may hold values from -6 to 6
- beta_weight: bfloat16 [32, 8192], P('head'), may hold values from -0.0625 to 0.0625
- decay_weight: bfloat16 [32, 8192], P('head'), may hold values from -0.0625 to 0.0625
- log_rate: float32 [32], P('head'), may hold values from -11.5 to -3
- decay_bias: float32 [32], P('head'), may hold values from -2 to 1
- delta_query: bfloat16 [4096, 4096], P('seq', 'head'), may hold values from -6 to 6
- delta_key: bfloat16 [4096, 4096], P('seq', 'head'), may hold values from -6 to 6
- delta_value: bfloat16 [4096, 4096], P('seq', 'head'), may hold values from -6 to 6
- delta_out_grad: bfloat16 [4096, 4096], P('seq', 'head'), may hold values from -6 to 6
- state_init: float32 [32, 128, 128], P('head'), may hold values from -6 to 6
- state_grad_next: float32 [32, 128, 128], P('head'), may hold values from -6 to 6
- attn_query: bfloat16 [4096, 1024], P('seq', 'head'), may hold values from -80 to 80
- attn_key: bfloat16 [4096, 1024], P('seq', 'head'), may hold values from -12 to 12
- attn_value: bfloat16 [4096, 1024], P('seq', 'head'), may hold values from -6 to 6
- attn_out_grad: bfloat16 [4096, 1024], P('seq', 'head'), may hold values from -6 to 6
Outputs:
- delta_query_grad: float32 [4096, 4096], P('seq', 'head')
- delta_key_grad: float32 [4096, 4096], P('seq', 'head')
- delta_value_grad: float32 [4096, 4096], P('seq', 'head')
- boundary_grads: float32 [32, 32, 128, 128], P('seq', 'head')
- input_grad: float32 [4096, 8192], P('seq', 'head')
- beta_weight_grad: float32 [32, 8192], P('head', 'seq')
- decay_weight_grad: float32 [32, 8192], P('head', 'seq')
- log_rate_grad: float32 [32], P('head')
- decay_bias_grad: float32 [32], P('head')
- attn_query_grad: float32 [4096, 1024], P('seq', 'head')
- attn_key_grad: float32 [4096, 1024], P('seq', 'head')
- attn_value_grad: float32 [4096, 1024], P('seq', 'head')
The draws below stay inside these ranges and needn't reach their ends.
All inputs are finite; a program needn't handle non-finite values.
Results may differ from the reference program's by a relative error of at most 0.00035.
Values may be sent and summed in bfloat16 or wider, within the bound.
No kernel may reach another device: no remote copies, remote signals or barrier semaphores. Data moves between devices by JAX's collectives and lax.ppermute only.
A program may use at most 128 MiB of HBM per device.

```python
import math
import jax
import jax.numpy as jnp
from jax import lax

D = 8192
HEADS = 32
DK = 128
DV = 128
STRETCH = 64
AHEADS = 8
AHD = 128
WINDOW = 1024
TOK_DEV = 128
TOKENS = 4096
N_SEQ = 32


def attention_pair(key):
    first_key, second_key = jax.random.split(jax.random.fold_in(key, 7))
    row_width = AHEADS * AHD
    queries = jnp.clip(jax.random.normal(first_key, (TOKENS, row_width), jnp.float32), -6.0, 6.0)
    key_rows = jnp.clip(jax.random.normal(second_key, (TOKENS, row_width), jnp.float32), -6.0, 6.0)
    return (queries, key_rows)


def draw_attn_query(key, part):
    return attention_pair(key)[0].astype(jnp.bfloat16)


def draw_attn_key(key, part):
    return attention_pair(key)[1].astype(jnp.bfloat16)


def draw_log_rate(key, part):
    slow_key, fast_key, pick_key = jax.random.split(jax.random.fold_in(key, 11), 3)
    slow = jax.random.uniform(slow_key, (HEADS,), jnp.float32, -11.5, -9.5)
    fast = jax.random.uniform(fast_key, (HEADS,), jnp.float32, -7.0, -3.0)
    share = 0.5
    picked = jax.random.uniform(pick_key, (HEADS,), jnp.float32) < share
    return jnp.where(picked, slow, fast)


def draw_delta_key(key, part):
    base_key, perm_key = jax.random.split(jax.random.fold_in(key, 13))
    base = jnp.clip(jax.random.normal(base_key, (TOKENS, HEADS, DK), jnp.float32), -6.0, 6.0)
    head_keys = jax.random.split(perm_key, HEADS)
    orders = jax.vmap(lambda one_key: jax.random.permutation(one_key, DK))(head_keys)
    inside = orders < max(DK // 8, 2)
    scales = jnp.where(inside, 1.0, 0.05).astype(jnp.float32)
    return (base * scales[None]).reshape(TOKENS, HEADS * DK).astype(jnp.bfloat16)


def level_of(rng, dims, cuts, smallest, high):
    gain, own = 1.0, jax.random.fold_in(rng, 6)
    for position, shards_of in cuts:
        heights = jnp.exp(jax.random.uniform(jax.random.fold_in(own, position), (shards_of,), jnp.float32, smallest / len(cuts), high / len(cuts)))
        gain = gain * jnp.repeat(heights, dims[position] // shards_of).reshape([-1 if axis == position else 1 for axis in range(len(dims))])
    return gain


def gaussian(own_key, extent, scale, limit, shards=(), kind=jnp.bfloat16):
    array = jax.random.normal(own_key, extent, jnp.float32) * scale
    if len(shards) > 0:
        array = level_of(own_key, extent, shards, -0.22, 0.18) * array
    return jnp.clip(array, min=-limit, max=limit).astype(kind)


def setup_inputs(seed: int = 0) -> dict:
    seeds = jax.random.split(jax.random.key(seed), 16)
    layer_input = gaussian(seeds[0], (TOKENS, D), 1.0, 6.0, ((0, 32),))
    beta_weight = gaussian(seeds[1], (HEADS, D), D ** -0.5, 0.0625, ((0, 8),))
    decay_weight = gaussian(seeds[2], (HEADS, D), D ** -0.5, 0.0625, ((0, 8),))
    log_rate = draw_log_rate(jax.random.fold_in(seeds[15], 71), 0)
    decay_bias = jnp.clip(-2.0 + 3.0 * jax.random.uniform(seeds[4], (HEADS,), jnp.float32) ** level_of(seeds[4], (HEADS,), ((0, 8),), -0.2, 0.2), -2.0, 1.0)
    delta_query = gaussian(seeds[5], (TOKENS, HEADS * DK), 1.0, 6.0, ((0, 32), (1, 8)))
    delta_key = draw_delta_key(jax.random.fold_in(seeds[15], 71), 0)
    delta_value = gaussian(seeds[7], (TOKENS, HEADS * DV), 1.0, 6.0, ((0, 32), (1, 8)))
    delta_out_grad = gaussian(seeds[8], (TOKENS, HEADS * DV), 1.0, 6.0, ((0, 32), (1, 8)))
    state_init = gaussian(seeds[9], (HEADS, DK, DV), 1.0, 6.0, ((0, 8),), jnp.float32)
    state_grad_next = gaussian(seeds[10], (HEADS, DK, DV), 1.0, 6.0, ((0, 8),), jnp.float32)
    attn_query = draw_attn_query(jax.random.fold_in(seeds[15], 71), 0)
    attn_key = draw_attn_key(jax.random.fold_in(seeds[15], 71), 0)
    attn_value = gaussian(seeds[13], (TOKENS, AHEADS * AHD), 1.0, 6.0, ((0, 32), (1, 8)))
    attn_out_grad = gaussian(seeds[14], (TOKENS, AHEADS * AHD), 1.0, 6.0, ((0, 32), (1, 8)))
    return {"layer_input": layer_input, "beta_weight": beta_weight, "decay_weight": decay_weight, "log_rate": log_rate, "decay_bias": decay_bias, "delta_query": delta_query, "delta_key": delta_key, "delta_value": delta_value, "delta_out_grad": delta_out_grad, "state_init": state_init, "state_grad_next": state_grad_next, "attn_query": attn_query, "attn_key": attn_key, "attn_value": attn_value, "attn_out_grad": attn_out_grad}


PRECISE = lax.Precision.HIGHEST

def dot_high(left_mat, right_mat):
    return jnp.matmul(left_mat, right_mat, precision=PRECISE)

def unit_rows(values):
    return values * lax.rsqrt(lax.optimization_barrier(jnp.sum(values * values, axis=-1, keepdims=True)) + 1e-06)

def stretch_step(memory, queries, key_rows, values, beta_rows, decay_log):
    span_len = queries.shape[0]
    cumulative = jnp.cumsum(decay_log)
    row_ids = lax.broadcasted_iota(jnp.int32, (span_len, span_len), 0)
    col_ids = lax.broadcasted_iota(jnp.int32, (span_len, span_len), 1)
    lower_mask = row_ids >= col_ids
    strict_mask = row_ids > col_ids
    ratios = jnp.where(lower_mask, jnp.exp(jnp.where(lower_mask, cumulative[:, None] - cumulative[None, :], 0.0)), 0.0)
    gram_keys = dot_high(key_rows, key_rows.T)
    system_mat = jnp.eye(span_len, dtype=queries.dtype) + jnp.where(strict_mask, beta_rows[:, None] * ratios * gram_keys, 0.0)
    growths = jnp.exp(cumulative)
    right_side = beta_rows[:, None] * (values - growths[:, None] * dot_high(key_rows, memory))
    updates = jax.scipy.linalg.solve_triangular(system_mat, right_side, lower=True, unit_diagonal=True)
    output = growths[:, None] * dot_high(queries, memory) + dot_high(ratios * dot_high(queries, key_rows.T), updates)
    tail_decay = jnp.exp(cumulative[-1] - cumulative)
    new_memory = jnp.exp(cumulative[-1]) * memory + dot_high((key_rows * tail_decay[:, None]).T, updates)
    return (new_memory, output)

def block_forward(memory, q_raw, k_raw, values, beta_rows, decay_rows):
    head_count, tok_count, key_width = q_raw.shape
    span_count = tok_count // STRETCH
    queries = unit_rows(q_raw) / math.sqrt(key_width)
    key_rows = unit_rows(k_raw)

    def in_stretches(array_in):
        return jnp.swapaxes(array_in.reshape((head_count, span_count, STRETCH) + array_in.shape[2:]), 0, 1)
    pieces_all = (in_stretches(queries), in_stretches(key_rows), in_stretches(values), in_stretches(beta_rows), in_stretches(decay_rows))
    stepper = jax.vmap(stretch_step)

    def advance(carried, pieces):
        return stepper(carried, pieces[0], pieces[1], pieces[2], pieces[3], pieces[4])
    final_mem, outputs = lax.scan(advance, memory, pieces_all)
    outputs = jnp.swapaxes(outputs, 0, 1).reshape(head_count, tok_count, values.shape[2])
    return (outputs, final_mem)

def gate_values(beta_logit, decay_input, log_rate, decay_bias):
    betas = jax.nn.sigmoid(beta_logit)
    decays = -jnp.exp(log_rate)[None, :] * jax.nn.softplus(decay_input + decay_bias[None, :])
    return (betas, decays)

def heads_first(flat_rows, head_count):
    return jnp.swapaxes(flat_rows.reshape(flat_rows.shape[0], head_count, -1), 0, 1)

def tokens_first(split_heads):
    return jnp.swapaxes(split_heads, 0, 1).reshape(split_heads.shape[1], -1)

def to_blocks(array_in):
    return jnp.swapaxes(array_in.reshape((array_in.shape[0], N_SEQ, TOK_DEV) + array_in.shape[2:]), 0, 1)

def segment_forward(q_raw, k_raw, v_raw, beta_logit, decay_input, log_rate, decay_bias, start_mem, bump_all):
    betas, decays = gate_values(beta_logit, decay_input, log_rate, decay_bias)
    pieces_all = (bump_all, to_blocks(q_raw), to_blocks(k_raw), to_blocks(v_raw), to_blocks(betas.T), to_blocks(decays.T))

    def one_block(memory, pieces):
        outputs, final_mem = block_forward(memory + pieces[0], pieces[1], pieces[2], pieces[3], pieces[4], pieces[5])
        return (final_mem, outputs)
    final_mem, outputs = lax.scan(one_block, start_mem, pieces_all)
    return (outputs, final_mem)

def attend(q_block, k_block, v_block, q_places, k_places):
    q_heads = q_block.reshape(q_block.shape[0], -1, AHD)
    k_heads = k_block.reshape(k_block.shape[0], -1, AHD)
    v_heads = v_block.reshape(v_block.shape[0], -1, AHD)
    scores = jnp.einsum('qhd,khd->hqk', q_heads, k_heads, precision=PRECISE) / math.sqrt(AHD)
    spread = q_places[:, None] - k_places[None, :]
    allowed = (spread >= 0) & (spread < WINDOW) & (k_places[None, :] >= 0)
    scores = jnp.where(allowed[None], scores, -1e+30)
    weights = jax.nn.softmax(scores, axis=-1)
    mixed = jnp.einsum('hqk,khd->qhd', weights, v_heads, precision=PRECISE)
    return mixed.reshape(q_block.shape[0], -1)

def window_backward(query_all, key_all, value_all, grad_all):
    row_width = query_all.shape[1]
    padding = jnp.zeros((WINDOW, row_width), jnp.float32)
    key_pad = jnp.concatenate([padding, key_all], axis=0)
    value_pad = jnp.concatenate([padding, value_all], axis=0)
    key_span = WINDOW + TOK_DEV

    def one_block(carried, block_id):
        key_acc, value_acc = carried
        start_row = (block_id * TOK_DEV).astype(jnp.int32)
        q_places = start_row + lax.iota(jnp.int32, TOK_DEV)
        k_places = start_row - WINDOW + lax.iota(jnp.int32, key_span)

        def attend_here(q_block, k_block, v_block):
            return attend(q_block, k_block, v_block, q_places, k_places)
        q_block = lax.dynamic_slice_in_dim(query_all, start_row, TOK_DEV, 0)
        k_block = lax.dynamic_slice_in_dim(key_pad, start_row, key_span, 0)
        v_block = lax.dynamic_slice_in_dim(value_pad, start_row, key_span, 0)
        primal, pullback = jax.vjp(attend_here, q_block, k_block, v_block)
        grad_q, grad_k, grad_v = pullback(lax.dynamic_slice_in_dim(grad_all, start_row, TOK_DEV, 0))
        key_acc = lax.dynamic_update_slice_in_dim(key_acc, lax.dynamic_slice_in_dim(key_acc, start_row, key_span, 0) + grad_k, start_row, 0)
        value_acc = lax.dynamic_update_slice_in_dim(value_acc, lax.dynamic_slice_in_dim(value_acc, start_row, key_span, 0) + grad_v, start_row, 0)
        return ((key_acc, value_acc), grad_q)
    (key_acc, value_acc), grad_blocks = lax.scan(one_block, (jnp.zeros_like(key_pad), jnp.zeros_like(value_pad)), jnp.arange(N_SEQ, dtype=jnp.int32))
    return (grad_blocks.reshape(TOKENS, row_width), key_acc[WINDOW:], value_acc[WINDOW:])

def reference(layer_input, beta_weight, decay_weight, log_rate, decay_bias, delta_query, delta_key, delta_value, delta_out_grad, state_init, state_grad_next, attn_query, attn_key, attn_value, attn_out_grad):
    beta_logit = jnp.dot(layer_input.astype(jnp.float32), beta_weight.T.astype(jnp.float32), preferred_element_type=jnp.float32)
    decay_input = jnp.dot(layer_input.astype(jnp.float32), decay_weight.T.astype(jnp.float32), preferred_element_type=jnp.float32)
    q_raw = heads_first(delta_query.astype(jnp.float32), HEADS)
    k_raw = heads_first(delta_key.astype(jnp.float32), HEADS)
    v_raw = heads_first(delta_value.astype(jnp.float32), HEADS)
    bump_all = jnp.zeros((N_SEQ, HEADS, DK, DV), jnp.float32)
    primal, pullback = jax.vjp(segment_forward, q_raw, k_raw, v_raw, beta_logit, decay_input, log_rate, decay_bias, state_init, bump_all)
    cotangent = (to_blocks(heads_first(delta_out_grad.astype(jnp.float32), HEADS)), state_grad_next)
    gradients = pullback(cotangent)
    grad_logit_b = gradients[3]
    grad_logit_d = gradients[4]
    input_grad = dot_high(grad_logit_b, beta_weight.astype(jnp.float32)) + dot_high(grad_logit_d, decay_weight.astype(jnp.float32))
    input_rows = layer_input.astype(jnp.float32)
    beta_weight_grad = dot_high(grad_logit_b.T, input_rows)
    decay_weight_grad = dot_high(grad_logit_d.T, input_rows)
    attn_q_grad, attn_k_grad, attn_v_grad = window_backward(attn_query.astype(jnp.float32), attn_key.astype(jnp.float32), attn_value.astype(jnp.float32), attn_out_grad.astype(jnp.float32))
    return (tokens_first(gradients[0]), tokens_first(gradients[1]), tokens_first(gradients[2]), gradients[8], input_grad, beta_weight_grad, decay_weight_grad, gradients[5], gradients[6], attn_q_grad, attn_k_grad, attn_v_grad)
```

```python
import math

import jax
import jax.numpy as jnp
from jax import lax
from jax.experimental import pallas as pl
from jax.experimental.pallas import tpu as pltpu
from jax.sharding import Mesh
from jax.sharding import PartitionSpec as P

WINDOW = 1024
T = 128
SEQ = ("seq_0", "seq_1")
F32 = jnp.float32
BF16 = jnp.bfloat16
NN = (((1,), (0,)), ((), ()))
NT = (((1,), (1,)), ((), ()))
TN = (((0,), (0,)), ((), ()))


def split(value):
    high = value.astype(BF16)
    return high, (value - high.astype(F32)).astype(BF16)


def split3(value):
    high = value.astype(BF16)
    rest = value - high.astype(F32)
    mid = rest.astype(BF16)
    return high, mid, (rest - mid.astype(F32)).astype(BF16)


def mm(left, right, dims):
    lefts = left if isinstance(left, tuple) else (left,)
    rights = right if isinstance(right, tuple) else (right,)
    total = None
    for i, a in enumerate(lefts):
        for j, b in enumerate(rights):
            if i + j < max(len(lefts), len(rights)):
                term = lax.dot_general(a, b, dims, preferred_element_type=F32)
                total = term if total is None else total + term
    return total


def ids(shape):
    return (
        lax.broadcasted_iota(jnp.int32, shape, 0),
        lax.broadcasted_iota(jnp.int32, shape, 1),
    )


def place(columns, lane):
    result = jnp.zeros((T, T), F32)
    for at, column in enumerate(columns):
        result = jnp.where(lane == at, column, result)
    return result


def prepare_kernel(
    x_ref, w_ref, rate_ref, bias_ref, q_ref, k_ref, v_ref, g_ref,
    maps_ref, inv_ref, ratio_ref, rk_ref, p_ref, w_out_ref, y_ref, du_ref, rows_ref, cols_ref,
):
    heads = maps_ref.shape[0]
    row, lane = ids((T, T))
    lower, strict = row >= lane, row > lane
    eye = jnp.where(row == lane, 1.0, 0.0)
    logits = lax.dot_general(w_ref[...], x_ref[...], NT, preferred_element_type=F32)
    rates = jnp.concatenate([jnp.full((1, T), rate_ref[h], F32) for h in range(heads)], axis=0)
    biases = jnp.concatenate([jnp.full((1, T), bias_ref[h], F32) for h in range(heads)], axis=0)
    beta_row = jax.nn.sigmoid(logits[:heads])
    shifted = logits[heads:] + biases
    soft = jnp.maximum(shifted, 0.0) + jnp.log1p(jnp.exp(-jnp.abs(shifted)))
    decay_row = -jnp.exp(rates) * soft
    upper_ones = jnp.where(row <= lane, 1.0, 0.0).astype(BF16)
    cum_row = mm(split3(decay_row), upper_ones, NN)
    gate_slope = -jnp.exp(rates) * jax.nn.sigmoid(shifted)
    packed = jnp.concatenate(
        [beta_row, cum_row, jnp.zeros((T - 2 * heads, T), F32)], axis=0
    )
    turned = packed.T
    hs = range(heads)
    span = [slice(h * T, (h + 1) * T) for h in hs]
    k = [k_ref[:, span[h]] for h in hs]
    q = [q_ref[:, span[h]] for h in hs]
    v = [v_ref[:, span[h]] for h in hs]
    g = [g_ref[:, span[h]] for h in hs]
    beta_c = [turned[:, h : h + 1] for h in hs]
    cum_c = [turned[:, heads + h : heads + h + 1] for h in hs]
    norm_k, norm_q = [], []
    for h in hs:
        kf, qf = k[h].astype(F32), q[h].astype(F32)
        norm_k.append(lax.rsqrt(jnp.sum(kf * kf, axis=1, keepdims=True) + 1e-6))
        norm_q.append(
            lax.rsqrt(jnp.sum(qf * qf, axis=1, keepdims=True) + 1e-6)
        )
    norms = place(norm_k + norm_q, lane)
    norm_rows = norms.T
    norm_k_row = norm_rows[:heads]
    norm_q_row = norm_rows[heads : 2 * heads]
    last = cum_row[:, T - 1 : T]
    rows_ref[...] = jnp.concatenate(
        [beta_row, cum_row, norm_k_row, norm_q_row, decay_row, gate_slope], axis=0
    )
    col_list = beta_c + cum_c + norm_k + norm_q
    cols_ref[...] = place(col_list, lane)
    scale = 1.0 / math.sqrt(T)
    ratio, solve, low = [], [], []
    for h in hs:
        r = jnp.where(
            lower, jnp.exp(jnp.where(lower, cum_c[h] - cum_row[h : h + 1], 0.0)), 0.0
        )
        ratio.append(r)
        ratio_ref[h] = r
        kk = mm(k[h], k[h], NT) * norm_k[h] * norm_k_row[h : h + 1]
        rk = jnp.where(strict, r * kk, 0.0)
        rk_ref[h] = rk
        low.append(rk * beta_c[h])
    for h in hs:
        same = (row // 2) == (lane // 2)
        solve.append(jnp.where(same, -low[h], 0.0) + eye)
    size = 2
    while size < T:
        block = (row // (2 * size) == lane // (2 * size)) & (row // size != lane // size)
        parts = [split(s) for s in solve]
        corner = [split(jnp.where(block, low[h], 0.0)) for h in hs]
        inner = [split(mm(corner[h], parts[h], NN)) for h in hs]
        solve = [solve[h] - mm(parts[h], inner[h], NN) for h in hs]
        size *= 2
    for h in hs:
        inv_ref[h] = solve[h]
        grow_c, grow_row = jnp.exp(cum_c[h]), jnp.exp(cum_row[h : h + 1])
        end = last[h : h + 1]
        tail_c = jnp.exp(end - cum_c[h])
        bv = beta_row[h : h + 1]
        w = mm(split(solve[h] * bv), v[h], NN)
        y = mm(split(solve[h] * (bv * grow_row * norm_k_row[h : h + 1])), k[h], NN)
        w_out_ref[h] = w
        y_ref[h] = y
        p = ratio[h] * mm(q[h], k[h], NT) * (norm_q[h] * scale) * norm_k_row[h : h + 1]
        p_ref[h] = p
        du = mm(split(p), g[h], TN)
        du_ref[h] = du
        out_scale = tail_c * norm_k[h]
        maps_ref[h, 0] = jnp.exp(end) * eye - mm(k[h], split(out_scale * y), TN)
        maps_ref[h, 1] = mm(k[h], split(out_scale * w), TN)
        own = mm(q[h], split((grow_c * norm_q[h] * scale) * g[h].astype(F32)), TN)
        maps_ref[h, 2] = own - mm(split(y), split(du), TN)


def group_kernel(maps_ref, up_ref, down_ref):
    phi = [split(maps_ref[x, 0]) for x in range(4)]
    off = [maps_ref[x, 1] for x in range(4)]
    loc = [maps_ref[x, 2] for x in range(4)]
    first = split(mm(phi[1], phi[0], NN))
    second = split(mm(phi[3], phi[2], NN))
    off_a = mm(phi[1], split(off[0]), NN) + off[1]
    off_b = mm(phi[3], split(off[2]), NN) + off[3]
    loc_a = mm(phi[0], split(loc[1]), TN) + loc[0]
    loc_b = mm(phi[2], split(loc[3]), TN) + loc[2]
    whole = mm(second, first, NN)
    up_ref[0] = whole
    down_ref[0] = whole
    up_ref[1] = mm(second, split(off_a), NN) + off_b
    down_ref[1] = mm(first, split(loc_b), TN) + loc_a


def pair_kernel(at_ref, up_ref, down_ref, from_up_ref, from_down_ref, up_out_ref, down_out_ref):
    z, count = at_ref[0], at_ref[1]
    own = split(up_ref[0])
    has_up, has_down = z >= 1, z < count - 1
    up_out_ref[0] = jnp.where(has_up, mm(own, split(from_up_ref[0]), NN), up_ref[0])
    up_out_ref[1] = jnp.where(
        has_up, mm(own, split(from_up_ref[1]), NN) + up_ref[1], up_ref[1]
    )
    down_out_ref[0] = jnp.where(has_down, mm(split(from_down_ref[0]), own, NN), down_ref[0])
    down_out_ref[1] = jnp.where(
        has_down, mm(own, split(from_down_ref[1]), TN) + down_ref[1], down_ref[1]
    )


def reach_kernel(
    at_ref, start_ref, end_ref, up_ref, down_ref, from_up_ref, from_down_ref, leave_ref, enter_ref
):
    z, count, x = at_ref[0], at_ref[1], at_ref[2]
    start, end = start_ref[x], end_ref[x]
    ahead = mm(split(from_up_ref[0]), split(start), NN) + from_up_ref[1]
    state = jnp.where(z >= 2, ahead, start)
    leave_ref[...] = mm(split(up_ref[0]), split(state), NN) + up_ref[1]
    behind = mm(split(from_down_ref[0]), split(end), TN) + from_down_ref[1]
    grad = jnp.where(z < count - 2, behind, end)
    enter_ref[...] = mm(split(down_ref[0]), split(grad), TN) + down_ref[1]


def spread_kernel(
    at_ref, start_ref, end_ref, leave_ref, enter_ref, up2_ref, down2_ref, up1_ref, down1_ref,
    maps_ref, out_ref,
):
    z, count, x = at_ref[0], at_ref[1], at_ref[2]
    state = jnp.where(z >= 4, leave_ref[...], start_ref[x])
    grad = jnp.where(z < count - 4, enter_ref[...], end_ref[x])
    state_two = mm(split(up2_ref[0]), split(state), NN) + up2_ref[1]
    grad_two = mm(split(down2_ref[0]), split(grad), TN) + down2_ref[1]
    state = jnp.where(z >= 2, state_two, state)
    grad = jnp.where(z < count - 2, grad_two, grad)
    state_one = mm(split(up1_ref[0]), split(state), NN) + up1_ref[1]
    grad_one = mm(split(down1_ref[0]), split(grad), TN) + down1_ref[1]
    state = jnp.where(z >= 1, state_one, state)
    grad = jnp.where(z < count - 1, grad_one, grad)
    for step in range(4):
        back = 3 - step
        out_ref[step, 0] = state
        out_ref[back, 1] = grad
        if step < 3:
            state = mm(split(maps_ref[step, 0]), split(state), NN) + maps_ref[step, 1]
            grad = mm(split(maps_ref[back, 0]), split(grad), TN) + maps_ref[back, 2]


def finish_kernel(
    ends_ref, maps_ref, q_ref, k_ref, v_ref, g_ref, inv_ref, ratio_ref, rk_ref, p_ref, w_ref,
    y_ref, du_ref, rows_ref, cols_ref,
    dq_ref, dk_ref, dv_ref, bound_ref, logit_ref, param_ref,
):
    heads = maps_ref.shape[0]
    hs = range(heads)
    row, lane = ids((T, T))
    strict = row > lane
    scale = 1.0 / math.sqrt(T)
    cols, rows = cols_ref[...], rows_ref[...]
    decay_cols, beta_cols, decay_rows, ends = [], [], [], []
    for h in hs:
        span = slice(h * T, (h + 1) * T)
        q, k, g = q_ref[:, span], k_ref[:, span], g_ref[:, span]
        qf, kf, vf = q.astype(F32), k.astype(F32), v_ref[:, span].astype(F32)
        beta = cols[:, h : h + 1]
        cum = cols[:, heads + h : heads + h + 1]
        norm_k = cols[:, 2 * heads + h : 2 * heads + h + 1]
        norm_q = cols[:, 3 * heads + h : 3 * heads + h + 1]
        norm_k_row = rows[2 * heads + h : 2 * heads + h + 1]
        norm_q_row = rows[3 * heads + h : 3 * heads + h + 1]
        end = rows[heads + h : heads + h + 1, T - 1 : T]
        grow, tail = jnp.exp(cum), jnp.exp(end - cum)
        m0, d = ends_ref[h, 0], ends_ref[h, 1]
        m_parts, d_parts = split(m0), split(d)
        u = w_ref[h] - mm(split(y_ref[h]), m_parts, NN)
        du = du_ref[h] + (tail * norm_k) * mm(k, d_parts, NN)
        u_parts = split(u)
        db = mm(split(inv_ref[h]), split(du), TN)
        db_parts = split(db)
        bound_ref[0, h] = mm(split(maps_ref[h, 0]), d_parts, TN) + maps_ref[h, 2]
        km = norm_k * mm(k, m_parts, NN)
        z = vf - grow * km
        dv_ref[:, span] = beta * db
        kn = norm_k * kf
        qn = (norm_q * scale) * qf
        dkn = -(beta * grow) * mm(db_parts, m_parts, NT)
        da = jnp.where(strict, -mm(db_parts, u_parts, NT), 0.0)
        ratio = ratio_ref[h]
        rka = da * rk_ref[h]
        hm = beta * ratio * da
        dkn = dkn + mm(split((hm + hm.T) * norm_k_row), k, NN)
        dp = mm(g, u_parts, NT)
        ds = ratio * dp
        dqn = mm(split(ds * norm_k_row), k, NN)
        dkn = dkn + mm(split(ds * (norm_q * scale)), q, TN)
        dom = mm(g, m_parts, NT)
        dqn = dqn + grow * dom
        dkt = tail * mm(u_parts, d_parts, NT)
        dkn = dkn + dkt
        both = beta * rka + dp * p_ref[h]
        tails = dkt * kn
        decay_cols.append(
            jnp.sum(both + grow * (dom * qn - beta * (db * km)) - tails, axis=1, keepdims=True)
        )
        beta_cols.append(jnp.sum(db * z + rka, axis=1, keepdims=True))
        decay_rows.append(jnp.sum(both, axis=0, keepdims=True))
        last = jnp.sum(
            jnp.sum(jnp.exp(end) * (d * m0) + tails, axis=0, keepdims=True), axis=1, keepdims=True
        )
        ends.append(jnp.broadcast_to(last, (1, T)))
        dot_q = jnp.sum(qf * dqn, axis=1, keepdims=True)
        dot_k = jnp.sum(kf * dkn, axis=1, keepdims=True)
        dq_ref[:, span] = (norm_q * scale) * (dqn - qf * (norm_q * norm_q * dot_q))
        dk_ref[:, span] = norm_k * (dkn - kf * (norm_k * norm_k * dot_k))
    turned = place(decay_cols + beta_cols, lane).T
    lane_one = lane[:heads]
    dcum = turned[:heads] - jnp.concatenate(decay_rows, axis=0)
    dcum = dcum + jnp.where(lane_one == T - 1, jnp.concatenate(ends, axis=0), 0.0)
    lower_ones = jnp.where(row >= lane, 1.0, 0.0).astype(BF16)
    ddecay = mm(split3(dcum), lower_ones, NN)
    beta_row = rows[:heads]
    dbeta = turned[heads : 2 * heads] * beta_row * (1.0 - beta_row)
    dshift = ddecay * rows[5 * heads : 6 * heads]
    logit_ref[...] = jnp.concatenate([dbeta, dshift], axis=0)
    rate_sum = jnp.sum(ddecay * rows[4 * heads : 5 * heads], axis=1, keepdims=True)
    bias_sum = jnp.sum(dshift, axis=1, keepdims=True)
    param_ref[...] = jnp.broadcast_to(
        jnp.concatenate([rate_sum, bias_sum], axis=0), (2 * heads, T)
    )


def window_kernel(at_ref, q_ref, g_ref, kv_ref, dq_ref, dkv_ref):
    z, x = at_ref[0], at_ref[2]
    row, lane = ids((T, T))
    gap = row - lane
    scale = 1.0 / math.sqrt(T)
    q, g = q_ref[...], g_ref[...]
    scores, slopes = [], []
    tiles = [(a, b) for a in range(4) for b in range(3)]
    for a, b in tiles:
        spread = gap + (x - a + 4 * b) * T
        ok = (spread >= 0) & (spread < jnp.where(z >= b, WINDOW, 0))
        s = lax.dot_general(q, kv_ref[a, b, 0], NT, preferred_element_type=F32) * scale
        scores.append(jnp.where(ok, s, -1e30))
    top = scores[0]
    for s in scores[1:]:
        top = jnp.maximum(top, s)
    top = jnp.max(top, axis=1, keepdims=True)
    weights = [jnp.exp(s - top) for s in scores]
    total = weights[0]
    for w in weights[1:]:
        total = total + w
    total = 1.0 / jnp.sum(total, axis=1, keepdims=True)
    weights = [w * total for w in weights]
    terms = None
    for (a, b), w in zip(tiles, weights):
        slope = lax.dot_general(g, kv_ref[a, b, 1], NT, preferred_element_type=F32)
        slopes.append(slope)
        terms = w * slope if terms is None else terms + w * slope
    terms = jnp.sum(terms, axis=1, keepdims=True)
    dq = None
    for (a, b), w, slope in zip(tiles, weights, slopes):
        ds = split(w * (slope - terms) * scale)
        part = mm(ds, kv_ref[a, b, 0], NN)
        dq = part if dq is None else dq + part
        dkv_ref[a, b, 0] = mm(ds, q, TN)
        dkv_ref[a, b, 1] = mm(split(w), g, TN)
    dq_ref[...] = dq


def input_kernel(d_ref, w_ref, out_ref):
    high, low = split(d_ref[...])
    w = w_ref[...]
    out_ref[...] = lax.dot_general(high, w, TN, preferred_element_type=F32) + lax.dot_general(
        low, w, TN, preferred_element_type=F32
    )


def weight_kernel(d_ref, param_ref, x_ref, out_ref):
    high, low = split(d_ref[...])
    pieces = out_ref.shape[0]
    width = x_ref.shape[1] // pieces
    for s in range(pieces):
        x = x_ref[:, s * width : (s + 1) * width]
        out_ref[s, :, :width] = lax.dot_general(
            high, x, NN, preferred_element_type=F32
        ) + lax.dot_general(low, x, NN, preferred_element_type=F32)
        out_ref[s, :, width:] = param_ref[...]


VM = pl.BlockSpec(memory_space=pltpu.VMEM)
SM = pl.BlockSpec(memory_space=pltpu.SMEM)


def f32(*shape):
    return jax.ShapeDtypeStruct(shape, F32)


def call(kernel, outs, specs, *args, flops=10**8):
    return pl.pallas_call(
        kernel,
        out_shape=outs,
        in_specs=specs,
        out_specs=jax.tree.map(lambda _: VM, outs),
        cost_estimate=pl.CostEstimate(flops=flops, bytes_accessed=4 * 10**6, transcendentals=0),
    )(*args)


def up_by(value, by, count):
    pairs = [(i, i + by) for i in range(count) if 0 <= i + by < count]
    return lax.ppermute(value, "seq_0", pairs)


def shards(
    layer_input, beta_weight, decay_weight, log_rate, decay_bias, delta_query, delta_key,
    delta_value, delta_out_grad, state_init, state_grad_next, attn_query, attn_key, attn_value,
    attn_out_grad,
):
    z_count, x_count = lax.axis_size("seq_0"), lax.axis_size("seq_1")
    head_count = lax.axis_size("head")
    heads = beta_weight.shape[0]
    width = layer_input.shape[1]
    at = jnp.stack(
        [lax.axis_index("seq_0"), jnp.int32(z_count), lax.axis_index("seq_1")]
    ).astype(jnp.int32)

    pair = jnp.stack([attn_key, attn_value])
    near, far = up_by(pair, 1, z_count), up_by(pair, 2, z_count)
    both_weights = jnp.concatenate([beta_weight, decay_weight], axis=0)

    maps, inv, ratio, rk, p, w, y, du, rows, cols = call(
        prepare_kernel,
        (f32(heads, 3, T, T),) + (f32(heads, T, T),) * 7 + (f32(6 * heads, T), f32(T, T)),
        [VM, VM, SM, SM, VM, VM, VM, VM],
        layer_input, both_weights, log_rate, decay_bias, delta_query, delta_key, delta_value,
        delta_out_grad,
    )
    blocks = lax.all_to_all(maps, "seq_1", split_axis=0, concat_axis=0, tiled=True)

    triple = jnp.stack([pair, near, far])
    copies = jnp.broadcast_to(triple[None], (x_count, *triple.shape))
    window = lax.all_to_all(copies, "seq_1", split_axis=0, concat_axis=0, tiled=True)
    weight_cols = jnp.swapaxes(both_weights.reshape(2 * heads, head_count, -1), 0, 1)
    weight_cols = lax.all_to_all(weight_cols, "head", split_axis=0, concat_axis=0, tiled=True)
    weight_cols = weight_cols.reshape(head_count * 2 * heads, -1)

    dq_attn, dkv = call(
        window_kernel,
        (f32(T, T), f32(x_count, 3, 2, T, T)),
        [SM, VM, VM, VM],
        at, attn_query, attn_out_grad, window,
    )

    up, down = call(group_kernel, (f32(2, T, T), f32(2, T, T)), [VM], blocks)
    up1, down1 = up_by(up, 1, z_count), up_by(down, -1, z_count)
    up, down = call(
        pair_kernel, (f32(2, T, T), f32(2, T, T)), [SM, VM, VM, VM, VM], at, up, down, up1, down1
    )
    up2, down2 = up_by(up, 2, z_count), up_by(down, -2, z_count)
    leave, enter = call(
        reach_kernel,
        (f32(T, T), f32(T, T)),
        [SM, VM, VM, VM, VM, VM, VM],
        at, state_init, state_grad_next, up, down, up2, down2,
    )
    leave, enter = up_by(leave, 4, z_count), up_by(enter, -4, z_count)
    ends = call(
        spread_kernel,
        f32(x_count, 2, T, T),
        [SM] + [VM] * 9,
        at, state_init, state_grad_next, leave, enter, up2, down2, up1, down1, blocks,
    )
    ends = lax.all_to_all(ends, "seq_1", split_axis=0, concat_axis=0, tiled=True)

    dkv = lax.all_to_all(dkv, "seq_1", split_axis=0, concat_axis=0, tiled=True)
    dkv = jnp.sum(dkv, axis=0)
    dkv_near, dkv_far = up_by(dkv[1], -1, z_count), up_by(dkv[2], -2, z_count)

    dq, dk, dv, bound, logit, param = call(
        finish_kernel,
        (f32(T, heads * T),) * 3 + (f32(1, heads, T, T), f32(2 * heads, T), f32(2 * heads, T)),
        [VM] * 15,
        ends, maps, delta_query, delta_key, delta_value, delta_out_grad, inv, ratio, rk, p, w, y,
        du, rows, cols,
    )
    logit_copies = jnp.broadcast_to(logit[None], (head_count, *logit.shape))
    every = lax.all_to_all(logit_copies, "head", split_axis=0, concat_axis=0, tiled=True)
    pieces = z_count * x_count
    terms = call(
        weight_kernel,
        f32(pieces, 2 * heads, width // pieces + T),
        [VM, VM, VM],
        logit, param, layer_input,
    )
    terms = lax.all_to_all(terms, SEQ, split_axis=0, concat_axis=0, tiled=True)
    input_grad = call(
        input_kernel,
        f32(T, weight_cols.shape[1]),
        [VM, VM],
        every.reshape(-1, T), weight_cols,
    )
    terms = jnp.sum(terms, axis=0)
    part = width // pieces
    total = dkv[0] + dkv_near + dkv_far
    return (
        dq, dk, dv, bound, input_grad,
        terms[:heads, :part], terms[heads:, :part],
        terms[:heads, part], terms[heads:, part],
        dq_attn, total[0], total[1],
    )


def solution(mesh):
    torus = Mesh(mesh.devices.reshape(8, 4, mesh.shape["head"]), ("seq_0", "seq_1", "head"))
    tokens, by_head = P(SEQ, "head"), P("head", None, None)
    in_specs = (
        P(SEQ, None), P("head", None), P("head", None), P("head"), P("head"),
        tokens, tokens, tokens, tokens, by_head, by_head, tokens, tokens, tokens, tokens,
    )
    out_specs = (
        tokens, tokens, tokens, P(SEQ, "head", None, None), tokens,
        P("head", SEQ), P("head", SEQ), P("head"), P("head"), tokens, tokens, tokens,
    )
    return jax.shard_map(
        shards, mesh=torus, in_specs=in_specs, out_specs=out_specs, check_vma=False
    )
```

```python
import math

import jax
import jax.numpy as jnp
from jax import lax
from jax.experimental import pallas as pl
from jax.experimental.pallas import tpu as pltpu
from jax.sharding import Mesh
from jax.sharding import PartitionSpec as P


WINDOW = 1024
T = 128
SEQ = ("seq_0", "seq_1")
F32 = jnp.float32
BF16 = jnp.bfloat16
NN = (((1,), (0,)), ((), ()))
NT = (((1,), (1,)), ((), ()))
TN = (((0,), (0,)), ((), ()))


def split(value):
    high = value.astype(BF16)
    return high, (value - high.astype(F32)).astype(BF16)


def split3(value):
    high = value.astype(BF16)
    rest = value - high.astype(F32)
    mid = rest.astype(BF16)
    return high, mid, (rest - mid.astype(F32)).astype(BF16)


def mm(left, right, dims):
    lefts = left if isinstance(left, tuple) else (left,)
    rights = right if isinstance(right, tuple) else (right,)
    total = None
    for i, a in enumerate(lefts):
        for j, b in enumerate(rights):
            if i + j < max(len(lefts), len(rights)):
                term = lax.dot_general(a, b, dims, preferred_element_type=F32)
                total = term if total is None else total + term
    return total


def ids(shape):
    return (
        lax.broadcasted_iota(jnp.int32, shape, 0),
        lax.broadcasted_iota(jnp.int32, shape, 1),
    )


def place(columns, lane):
    result = jnp.zeros((T, T), F32)
    for at, column in enumerate(columns):
        result = jnp.where(lane == at, column, result)
    return result


def prepare_kernel(
    x_ref, w_ref, rate_ref, bias_ref, q_ref, k_ref, v_ref, g_ref,
    maps_ref, inv_ref, ratio_ref, rk_ref, p_ref, w_out_ref, y_ref, du_ref, rows_ref, cols_ref,
):
    heads = maps_ref.shape[0]
    row, lane = ids((T, T))
    lower, strict = row >= lane, row > lane
    eye = jnp.where(row == lane, 1.0, 0.0)
    logits = lax.dot_general(w_ref[...], x_ref[...], NT, preferred_element_type=F32)
    rates = jnp.concatenate([jnp.full((1, T), rate_ref[h], F32) for h in range(heads)], axis=0)
    biases = jnp.concatenate([jnp.full((1, T), bias_ref[h], F32) for h in range(heads)], axis=0)
    beta_row = jax.nn.sigmoid(logits[:heads])
    shifted = logits[heads:] + biases
    soft = jnp.maximum(shifted, 0.0) + jnp.log1p(jnp.exp(-jnp.abs(shifted)))
    decay_row = -jnp.exp(rates) * soft
    upper_ones = jnp.where(row <= lane, 1.0, 0.0).astype(BF16)
    cum_row = mm(split3(decay_row), upper_ones, NN)
    gate_slope = -jnp.exp(rates) * jax.nn.sigmoid(shifted)
    packed = jnp.concatenate(
        [beta_row, cum_row, jnp.zeros((T - 2 * heads, T), F32)], axis=0
    )
    turned = packed.T
    hs = range(heads)
    span = [slice(h * T, (h + 1) * T) for h in hs]
    k = [k_ref[:, span[h]] for h in hs]
    q = [q_ref[:, span[h]] for h in hs]
    v = [v_ref[:, span[h]] for h in hs]
    g = [g_ref[:, span[h]] for h in hs]
    beta_c = [turned[:, h : h + 1] for h in hs]
    cum_c = [turned[:, heads + h : heads + h + 1] for h in hs]
    norm_k, norm_q = [], []
    for h in hs:
        kf, qf = k[h].astype(F32), q[h].astype(F32)
        norm_k.append(lax.rsqrt(jnp.sum(kf * kf, axis=1, keepdims=True) + 1e-6))
        norm_q.append(
            lax.rsqrt(jnp.sum(qf * qf, axis=1, keepdims=True) + 1e-6)
        )
    norms = place(norm_k + norm_q, lane)
    norm_rows = norms.T
    norm_k_row = norm_rows[:heads]
    norm_q_row = norm_rows[heads : 2 * heads]
    last = cum_row[:, T - 1 : T]
    rows_ref[...] = jnp.concatenate(
        [beta_row, cum_row, norm_k_row, norm_q_row, decay_row, gate_slope], axis=0
    )
    col_list = beta_c + cum_c + norm_k + norm_q
    cols_ref[...] = place(col_list, lane)
    scale = 1.0 / math.sqrt(T)
    ratio, solve, low = [], [], []
    for h in hs:
        r = jnp.where(
            lower, jnp.exp(jnp.where(lower, cum_c[h] - cum_row[h : h + 1], 0.0)), 0.0
        )
        ratio.append(r)
        ratio_ref[h] = r
        kk = mm(k[h], k[h], NT) * norm_k[h] * norm_k_row[h : h + 1]
        rk = jnp.where(strict, r * kk, 0.0)
        rk_ref[h] = rk
        low.append(rk * beta_c[h])
    for h in hs:
        same = (row // 2) == (lane // 2)
        solve.append(jnp.where(same, -low[h], 0.0) + eye)
    size = 2
    while size < T:
        block = (row // (2 * size) == lane // (2 * size)) & (row // size != lane // size)
        parts = [split(s) for s in solve]
        corner = [split(jnp.where(block, low[h], 0.0)) for h in hs]
        inner = [split(mm(corner[h], parts[h], NN)) for h in hs]
        solve = [solve[h] - mm(parts[h], inner[h], NN) for h in hs]
        size *= 2
    for h in hs:
        inv_ref[h] = solve[h]
        grow_c, grow_row = jnp.exp(cum_c[h]), jnp.exp(cum_row[h : h + 1])
        end = last[h : h + 1]
        tail_c = jnp.exp(end - cum_c[h])
        bv = beta_row[h : h + 1]
        w = mm(split(solve[h] * bv), v[h], NN)
        y = mm(split(solve[h] * (bv * grow_row * norm_k_row[h : h + 1])), k[h], NN)
        w_out_ref[h] = w
        y_ref[h] = y
        p = ratio[h] * mm(q[h], k[h], NT) * (norm_q[h] * scale) * norm_k_row[h : h + 1]
        p_ref[h] = p
        du = mm(split(p), g[h], TN)
        du_ref[h] = du
        out_scale = tail_c * norm_k[h]
        maps_ref[h, 0] = jnp.exp(end) * eye - mm(k[h], split(out_scale * y), TN)
        maps_ref[h, 1] = mm(k[h], split(out_scale * w), TN)
        own = mm(q[h], split((grow_c * norm_q[h] * scale) * g[h].astype(F32)), TN)
        maps_ref[h, 2] = own - mm(split(y), split(du), TN)


def group_kernel(at_ref, maps_ref, out_ref):
    z = at_ref[0]
    phi = [split(maps_ref[x, 0]) for x in range(4)]
    off = [maps_ref[x, 1] for x in range(4)]
    loc = [maps_ref[x, 2] for x in range(4)]
    first = split(mm(phi[1], phi[0], NN))
    second = split(mm(phi[3], phi[2], NN))
    off_a = mm(phi[1], split(off[0]), NN) + off[1]
    off_b = mm(phi[3], split(off[2]), NN) + off[3]
    loc_a = mm(phi[0], split(loc[1]), TN) + loc[0]
    loc_b = mm(phi[2], split(loc[3]), TN) + loc[2]
    whole = mm(second, first, NN)
    later = mm(second, split(off_a), NN) + off_b
    earlier = mm(first, split(loc_b), TN) + loc_a
    for to in range(out_ref.shape[0]):
        out_ref[to, 0] = whole
        out_ref[to, 1] = jnp.where(to > z, later, earlier)


def spread_kernel(at_ref, start_ref, end_ref, groups_ref, maps_ref, out_ref):
    z, x = at_ref[0], at_ref[1]
    count = groups_ref.shape[0]
    state, grad = start_ref[x], end_ref[x]
    for step in range(count - 1):
        back = count - 1 - step
        ahead = mm(split(groups_ref[step, 0]), split(state), NN) + groups_ref[step, 1]
        behind = mm(split(groups_ref[back, 0]), split(grad), TN) + groups_ref[back, 1]
        state = jnp.where(step < z, ahead, state)
        grad = jnp.where(back > z, behind, grad)
    for step in range(4):
        back = 3 - step
        out_ref[step, 0] = state
        out_ref[back, 1] = grad
        if step < 3:
            state = mm(split(maps_ref[step, 0]), split(state), NN) + maps_ref[step, 1]
            grad = mm(split(maps_ref[back, 0]), split(grad), TN) + maps_ref[back, 2]


def finish_kernel(
    ends_ref, maps_ref, q_ref, k_ref, v_ref, g_ref, inv_ref, ratio_ref, rk_ref, p_ref, w_ref,
    y_ref, du_ref, rows_ref, cols_ref,
    dq_ref, dk_ref, dv_ref, bound_ref, logit_ref, param_ref,
):
    heads = maps_ref.shape[0]
    hs = range(heads)
    row, lane = ids((T, T))
    strict = row > lane
    scale = 1.0 / math.sqrt(T)
    cols, rows = cols_ref[...], rows_ref[...]
    decay_cols, beta_cols, decay_rows, ends = [], [], [], []
    for h in hs:
        span = slice(h * T, (h + 1) * T)
        q, k, g = q_ref[:, span], k_ref[:, span], g_ref[:, span]
        qf, kf, vf = q.astype(F32), k.astype(F32), v_ref[:, span].astype(F32)
        beta = cols[:, h : h + 1]
        cum = cols[:, heads + h : heads + h + 1]
        norm_k = cols[:, 2 * heads + h : 2 * heads + h + 1]
        norm_q = cols[:, 3 * heads + h : 3 * heads + h + 1]
        norm_k_row = rows[2 * heads + h : 2 * heads + h + 1]
        end = rows[heads + h : heads + h + 1, T - 1 : T]
        grow, tail = jnp.exp(cum), jnp.exp(end - cum)
        m0, d = ends_ref[h, 0], ends_ref[h, 1]
        m_parts, d_parts = split(m0), split(d)
        u = w_ref[h] - mm(split(y_ref[h]), m_parts, NN)
        du = du_ref[h] + (tail * norm_k) * mm(k, d_parts, NN)
        u_parts = split(u)
        db = mm(split(inv_ref[h]), split(du), TN)
        db_parts = split(db)
        bound_ref[0, h] = mm(split(maps_ref[h, 0]), d_parts, TN) + maps_ref[h, 2]
        km = norm_k * mm(k, m_parts, NN)
        z = vf - grow * km
        dv_ref[:, span] = beta * db
        kn = norm_k * kf
        qn = (norm_q * scale) * qf
        dkn = -(beta * grow) * mm(db_parts, m_parts, NT)
        da = jnp.where(strict, -mm(db_parts, u_parts, NT), 0.0)
        ratio = ratio_ref[h]
        rka = da * rk_ref[h]
        hm = beta * ratio * da
        dkn = dkn + mm(split((hm + hm.T) * norm_k_row), k, NN)
        dp = mm(g, u_parts, NT)
        ds = ratio * dp
        dqn = mm(split(ds * norm_k_row), k, NN)
        dkn = dkn + mm(split(ds * (norm_q * scale)), q, TN)
        dom = mm(g, m_parts, NT)
        dqn = dqn + grow * dom
        dkt = tail * mm(u_parts, d_parts, NT)
        dkn = dkn + dkt
        both = beta * rka + dp * p_ref[h]
        tails = dkt * kn
        decay_cols.append(
            jnp.sum(both + grow * (dom * qn - beta * (db * km)) - tails, axis=1, keepdims=True)
        )
        beta_cols.append(jnp.sum(db * z + rka, axis=1, keepdims=True))
        decay_rows.append(jnp.sum(both, axis=0, keepdims=True))
        last = jnp.sum(
            jnp.sum(jnp.exp(end) * (d * m0) + tails, axis=0, keepdims=True), axis=1, keepdims=True
        )
        ends.append(jnp.broadcast_to(last, (1, T)))
        dot_q = jnp.sum(qf * dqn, axis=1, keepdims=True)
        dot_k = jnp.sum(kf * dkn, axis=1, keepdims=True)
        dq_ref[:, span] = (norm_q * scale) * (dqn - qf * (norm_q * norm_q * dot_q))
        dk_ref[:, span] = norm_k * (dkn - kf * (norm_k * norm_k * dot_k))
    turned = place(decay_cols + beta_cols, lane).T
    lane_one = lane[:heads]
    dcum = turned[:heads] - jnp.concatenate(decay_rows, axis=0)
    dcum = dcum + jnp.where(lane_one == T - 1, jnp.concatenate(ends, axis=0), 0.0)
    lower_ones = jnp.where(row >= lane, 1.0, 0.0).astype(BF16)
    ddecay = mm(split3(dcum), lower_ones, NN)
    beta_row = rows[:heads]
    dbeta = turned[heads : 2 * heads] * beta_row * (1.0 - beta_row)
    dshift = ddecay * rows[5 * heads : 6 * heads]
    logit_ref[...] = jnp.concatenate([dbeta, dshift], axis=0)
    rate_sum = jnp.sum(ddecay * rows[4 * heads : 5 * heads], axis=1, keepdims=True)
    bias_sum = jnp.sum(dshift, axis=1, keepdims=True)
    param_ref[...] = jnp.broadcast_to(
        jnp.concatenate([rate_sum, bias_sum], axis=0), (2 * heads, T)
    )


def window_kernel(at_ref, q_ref, g_ref, *refs):
    kv_refs, dq_ref, dkv_refs = refs[:4], refs[4], refs[5:]
    z, x = at_ref[0], at_ref[1]
    row, lane = ids((T, T))
    gap = row - lane
    scale = 1.0 / math.sqrt(T)
    q, g = q_ref[...], g_ref[...]
    scores, slopes = [], []
    tiles = [(a, b) for a in range(4) for b in range(3)]
    for a, b in tiles:
        spread = gap + (jnp.where(x >= a, a, a - 4) + 4 * b) * T
        ok = (spread >= 0) & (spread < jnp.where(z >= b, WINDOW, 0))
        s = lax.dot_general(q, kv_refs[a][b, 0], NT, preferred_element_type=F32) * scale
        scores.append(jnp.where(ok, s, -1e30))
    top = scores[0]
    for s in scores[1:]:
        top = jnp.maximum(top, s)
    top = jnp.max(top, axis=1, keepdims=True)
    weights = [jnp.exp(s - top) for s in scores]
    total = weights[0]
    for w in weights[1:]:
        total = total + w
    total = 1.0 / jnp.sum(total, axis=1, keepdims=True)
    weights = [w * total for w in weights]
    terms = None
    for (a, b), w in zip(tiles, weights):
        slope = lax.dot_general(g, kv_refs[a][b, 1], NT, preferred_element_type=F32)
        slopes.append(slope)
        terms = w * slope if terms is None else terms + w * slope
    terms = jnp.sum(terms, axis=1, keepdims=True)
    dq = None
    for (a, b), w, slope in zip(tiles, weights, slopes):
        ds = split(w * (slope - terms) * scale)
        part = mm(ds, kv_refs[a][b, 0], NN)
        dq = part if dq is None else dq + part
        dkv_refs[a][b, 0] = mm(ds, q, TN)
        dkv_refs[a][b, 1] = mm(split(w), g, TN)
    dq_ref[...] = dq


def input_kernel(at_ref, w_ref, *refs):
    rows_refs, out_ref, all_ref = refs[:-2], refs[-2], refs[-1]
    head, count = at_ref[2], len(rows_refs)
    for d, rows_ref in enumerate(rows_refs):
        source = jnp.where(head >= d, head - d, head - d + count)
        all_ref[pl.ds(pl.multiple_of(source * 8, 8), 8), :] = rows_ref[...]
    high, low = split(all_ref[...])
    w = w_ref[...]
    out_ref[...] = lax.dot_general(high, w, TN, preferred_element_type=F32) + lax.dot_general(
        low, w, TN, preferred_element_type=F32
    )


def weight_kernel(d_ref, param_ref, x_ref, out_ref):
    high, low = split(d_ref[...])
    pieces = out_ref.shape[0]
    width = x_ref.shape[1] // pieces
    for s in range(pieces):
        x = x_ref[:, s * width : (s + 1) * width]
        out_ref[s, :, :width] = lax.dot_general(
            high, x, NN, preferred_element_type=F32
        ) + lax.dot_general(low, x, NN, preferred_element_type=F32)
        out_ref[s, :, width:] = param_ref[...]


VM = pl.BlockSpec(memory_space=pltpu.VMEM)
SM = pl.BlockSpec(memory_space=pltpu.SMEM)


def f32(*shape):
    return jax.ShapeDtypeStruct(shape, F32)


def call(kernel, outs, specs, *args, flops=10**8, scratch=(), limit=24 * 2**20):
    return run(kernel, outs, specs, args, flops, scratch, limit)


def exchange(value, axis):
    return lax.all_to_all(value, axis, split_axis=0, concat_axis=0, tiled=True)


def run(kernel, outs, specs, args, flops, scratch, limit):
    return pl.pallas_call(
        kernel,
        out_shape=outs,
        in_specs=specs,
        out_specs=jax.tree.map(lambda _: VM, outs),
        scratch_shapes=scratch,
        cost_estimate=pl.CostEstimate(flops=flops, bytes_accessed=4 * 10**6, transcendentals=0),
        compiler_params=pltpu.CompilerParams(vmem_limit_bytes=limit),
    )(*args)


WHOLE = 60 * 1024 * 1024


def up_by(value, by, count):
    pairs = [(i, i + by) for i in range(count) if 0 <= i + by < count]
    return lax.ppermute(value, "seq_0", pairs)


def turn(value, axis, by, count):
    return lax.ppermute(value, axis, [(i, (i + by) % count) for i in range(count)])


def shards(
    layer_input, beta_weight, decay_weight, log_rate, decay_bias, delta_query, delta_key,
    delta_value, delta_out_grad, state_init, state_grad_next, attn_query, attn_key, attn_value,
    attn_out_grad,
):
    z_count, x_count = lax.axis_size("seq_0"), lax.axis_size("seq_1")
    head_count = lax.axis_size("head")
    heads = beta_weight.shape[0]
    width = layer_input.shape[1]
    pieces = z_count * x_count
    at = jnp.stack(
        [lax.axis_index("seq_0"), lax.axis_index("seq_1"), lax.axis_index("head")]
    ).astype(jnp.int32)

    pair = jnp.stack([attn_key, attn_value])
    near, far = up_by(pair, 1, z_count), up_by(pair, 2, z_count)
    both_weights = jnp.concatenate([beta_weight, decay_weight], axis=0)
    weight_cols = jnp.swapaxes(both_weights.reshape(2 * heads, head_count, -1), 0, 1)
    weight_cols = exchange(weight_cols, "head")
    weight_cols = weight_cols.reshape(head_count * 2 * heads, -1)

    maps, inv, ratio, rk, p, w, y, du, rows, cols = call(
        prepare_kernel,
        (f32(heads, 3, T, T),) + (f32(heads, T, T),) * 7 + (f32(6 * heads, T), f32(T, T)),
        [VM, VM, SM, SM, VM, VM, VM, VM],
        layer_input, both_weights, log_rate, decay_bias, delta_query, delta_key, delta_value,
        delta_out_grad,
        limit=WHOLE,
    )
    maps, weight_cols = lax.optimization_barrier((maps, weight_cols))
    blocks = exchange(maps, "seq_1")
    groups = call(group_kernel, f32(z_count, 2, T, T), [SM, VM], at, blocks)

    triple = jnp.stack([pair, near, far])
    triple, groups = lax.optimization_barrier((triple, groups))
    groups = exchange(groups, "seq_0")
    windows = [triple] + [turn(triple, "seq_1", d, x_count) for d in range(1, x_count)]
    dq_attn, *dkv = call(
        window_kernel,
        (f32(T, T),) + (f32(3, 2, T, T),) * x_count,
        [SM] + [VM] * (2 + x_count),
        at, attn_query, attn_out_grad, *windows,
    )
    dkv = [dkv[0]] + [turn(dkv[d], "seq_1", -d, x_count) for d in range(1, x_count)]

    ends = call(
        spread_kernel,
        f32(x_count, 2, T, T),
        [SM] + [VM] * 4,
        at, state_init, state_grad_next, groups, blocks,
    )
    ends = exchange(ends, "seq_1")

    dq, dk, dv, bound, logit, param = call(
        finish_kernel,
        (f32(T, heads * T),) * 3 + (f32(1, heads, T, T), f32(2 * heads, T), f32(2 * heads, T)),
        [VM] * 15,
        ends, maps, delta_query, delta_key, delta_value, delta_out_grad, inv, ratio, rk, p, w, y,
        du, rows, cols,
        limit=WHOLE,
    )
    terms = call(
        weight_kernel,
        f32(pieces, 2 * heads, width // pieces + T),
        [VM, VM, VM],
        logit, param, layer_input,
    )
    terms, logit = lax.optimization_barrier((terms, logit))
    terms = exchange(terms, SEQ)
    every = [logit] + [turn(logit, "head", d, head_count) for d in range(1, head_count)]
    dkv = sum(dkv[1:], dkv[0])
    dkv_near, dkv_far = up_by(dkv[1], -1, z_count), up_by(dkv[2], -2, z_count)
    input_grad = call(
        input_kernel,
        f32(T, weight_cols.shape[1]),
        [SM] + [VM] * (1 + head_count),
        at, weight_cols, *every,
        scratch=[pltpu.VMEM((2 * heads * head_count, T), F32)],
    )
    terms = jnp.sum(terms, axis=0)
    part = width // pieces
    total = dkv[0] + dkv_near + dkv_far
    return (
        dq, dk, dv, bound, input_grad,
        terms[:heads, :part], terms[heads:, :part],
        terms[:heads, part], terms[heads:, part],
        dq_attn, total[0], total[1],
    )


def solution(mesh):
    torus = Mesh(mesh.devices.reshape(8, 4, mesh.shape["head"]), ("seq_0", "seq_1", "head"))
    tokens, by_head = P(SEQ, "head"), P("head", None, None)
    in_specs = (
        P(SEQ, None), P("head", None), P("head", None), P("head"), P("head"),
        tokens, tokens, tokens, tokens, by_head, by_head, tokens, tokens, tokens, tokens,
    )
    out_specs = (
        tokens, tokens, tokens, P(SEQ, "head", None, None), tokens,
        P("head", SEQ), P("head", SEQ), P("head"), P("head"), tokens, tokens, tokens,
    )

    return jax.shard_map(
        shards, mesh=torus, in_specs=in_specs, out_specs=out_specs, check_vma=False
    )
```

```python
import math

import jax
import jax.numpy as jnp
from jax import lax
from jax.experimental import pallas as pl
from jax.experimental.pallas import tpu as pltpu
from jax.sharding import Mesh
from jax.sharding import PartitionSpec as P


WINDOW = 1024
T = 128
SEQ = ("seq_0", "seq_1")
F32 = jnp.float32
BF16 = jnp.bfloat16
NN = (((1,), (0,)), ((), ()))
NT = (((1,), (1,)), ((), ()))
TN = (((0,), (0,)), ((), ()))


def split(value):
    high = value.astype(BF16)
    return high, (value - high.astype(F32)).astype(BF16)


def split3(value):
    high = value.astype(BF16)
    rest = value - high.astype(F32)
    mid = rest.astype(BF16)
    return high, mid, (rest - mid.astype(F32)).astype(BF16)


def mm(left, right, dims):
    lefts = left if isinstance(left, tuple) else (left,)
    rights = right if isinstance(right, tuple) else (right,)
    total = None
    for i, a in enumerate(lefts):
        for j, b in enumerate(rights):
            if i + j < max(len(lefts), len(rights)):
                term = lax.dot_general(a, b, dims, preferred_element_type=F32)
                total = term if total is None else total + term
    return total


def ids(shape):
    return (
        lax.broadcasted_iota(jnp.int32, shape, 0),
        lax.broadcasted_iota(jnp.int32, shape, 1),
    )


def place(columns, lane):
    result = jnp.zeros((T, T), F32)
    for at, column in enumerate(columns):
        result = jnp.where(lane == at, column, result)
    return result


def prepare_kernel(
    at_ref, x_hbm, wb_ref, wd_ref, rate_ref, bias_ref, q_ref, k_ref, v_ref, g_ref,
    maps_ref, inv_ref, ratio_ref, rk_ref, p_ref, w_out_ref, y_ref, du_ref, rows_ref, cols_ref,
    *rest,
):
    chunk_refs, (w_ref, x_ref, sem) = rest[:-3], rest[-3:]
    fetch = pltpu.make_async_copy(x_hbm, x_ref, sem)
    fetch.start()
    heads = maps_ref.shape[0]
    w_ref[...] = jnp.concatenate(
        [wb_ref[...].astype(F32), wd_ref[...].astype(F32)], axis=0
    ).astype(BF16)
    count = len(chunk_refs)
    size = w_ref.shape[1] // count
    for d, chunk_ref in enumerate(chunk_refs):
        to = at_ref[2] + d
        to = jnp.where(to >= count, to - count, to)
        chunk_ref[...] = w_ref[:, pl.ds(pl.multiple_of(to * size, size), size)]
    row, lane = ids((T, T))
    lower, strict = row >= lane, row > lane
    eye = jnp.where(row == lane, 1.0, 0.0)
    hs = range(heads)
    span = [slice(h * T, (h + 1) * T) for h in hs]
    k = [k_ref[:, span[h]] for h in hs]
    q = [q_ref[:, span[h]] for h in hs]
    v = [v_ref[:, span[h]] for h in hs]
    g = [g_ref[:, span[h]] for h in hs]
    norm_k, norm_q = [], []
    for h in hs:
        kf, qf = k[h].astype(F32), q[h].astype(F32)
        norm_k.append(lax.rsqrt(jnp.sum(kf * kf, axis=1, keepdims=True) + 1e-6))
        norm_q.append(lax.rsqrt(jnp.sum(qf * qf, axis=1, keepdims=True) + 1e-6))
    norm_rows = place(norm_k + norm_q, lane).T
    norm_k_row = norm_rows[:heads]
    norm_q_row = norm_rows[heads : 2 * heads]
    for h in hs:
        rk_ref[h] = mm(k[h], k[h], NT) * norm_k[h] * norm_k_row[h : h + 1]
        p_ref[h] = mm(q[h], k[h], NT) * (norm_q[h] * (1.0 / math.sqrt(T))) * norm_k_row[h : h + 1]
    rates = jnp.concatenate([jnp.full((1, T), rate_ref[h], F32) for h in hs], axis=0)
    biases = jnp.concatenate([jnp.full((1, T), bias_ref[h], F32) for h in hs], axis=0)
    fetch.wait()
    logits = lax.dot_general(w_ref[...], x_ref[...], NT, preferred_element_type=F32)
    beta_row = jax.nn.sigmoid(logits[:heads])
    shifted = logits[heads:] + biases
    soft = jnp.maximum(shifted, 0.0) + jnp.log1p(jnp.exp(-jnp.abs(shifted)))
    decay_row = -jnp.exp(rates) * soft
    upper_ones = jnp.where(row <= lane, 1.0, 0.0).astype(BF16)
    cum_row = mm(split3(decay_row), upper_ones, NN)
    gate_slope = -jnp.exp(rates) * jax.nn.sigmoid(shifted)
    turned = jnp.concatenate([beta_row, cum_row, jnp.zeros((T - 2 * heads, T), F32)], axis=0).T
    beta_c = [turned[:, h : h + 1] for h in hs]
    cum_c = [turned[:, heads + h : heads + h + 1] for h in hs]
    last = cum_row[:, T - 1 : T]
    rows_ref[...] = jnp.concatenate(
        [beta_row, cum_row, norm_k_row, norm_q_row, decay_row, gate_slope], axis=0
    )
    cols_ref[...] = place(beta_c + cum_c + norm_k + norm_q, lane)
    scale = 1.0 / math.sqrt(T)
    ratio, solve, low = [], [], []
    for h in hs:
        r = jnp.where(
            lower, jnp.exp(jnp.where(lower, cum_c[h] - cum_row[h : h + 1], 0.0)), 0.0
        )
        ratio.append(r)
        ratio_ref[h] = r
        rk = jnp.where(strict, r * rk_ref[h], 0.0)
        rk_ref[h] = rk
        low.append(rk * beta_c[h])
    for h in hs:
        same = (row // 2) == (lane // 2)
        solve.append(jnp.where(same, -low[h], 0.0) + eye)
    size = 2
    while size < T:
        block = (row // (2 * size) == lane // (2 * size)) & (row // size != lane // size)
        parts = [split(s) for s in solve]
        corner = [split(jnp.where(block, low[h], 0.0)) for h in hs]
        inner = [split(mm(corner[h], parts[h], NN)) for h in hs]
        solve = [solve[h] - mm(parts[h], inner[h], NN) for h in hs]
        size *= 2
    for h in hs:
        inv_ref[h] = solve[h]
        grow_c, grow_row = jnp.exp(cum_c[h]), jnp.exp(cum_row[h : h + 1])
        end = last[h : h + 1]
        tail_c = jnp.exp(end - cum_c[h])
        bv = beta_row[h : h + 1]
        w = mm(split(solve[h] * bv), v[h], NN)
        y = mm(split(solve[h] * (bv * grow_row * norm_k_row[h : h + 1])), k[h], NN)
        w_out_ref[h] = w
        y_ref[h] = y
        p = ratio[h] * p_ref[h]
        p_ref[h] = p
        du = mm(split(p), g[h], TN)
        du_ref[h] = du
        out_scale = tail_c * norm_k[h]
        maps_ref[h, 0] = jnp.exp(end) * eye - mm(k[h], split(out_scale * y), TN)
        maps_ref[h, 1] = mm(k[h], split(out_scale * w), TN)
        own = mm(q[h], split((grow_c * norm_q[h] * scale) * g[h].astype(F32)), TN)
        maps_ref[h, 2] = own - mm(split(y), split(du), TN)


def group_kernel(at_ref, maps_ref, out_ref):
    z = at_ref[0]
    phi = [split(maps_ref[x, 0]) for x in range(4)]
    off = [maps_ref[x, 1] for x in range(4)]
    loc = [maps_ref[x, 2] for x in range(4)]
    first = split(mm(phi[1], phi[0], NN))
    second = split(mm(phi[3], phi[2], NN))
    off_a = mm(phi[1], split(off[0]), NN) + off[1]
    off_b = mm(phi[3], split(off[2]), NN) + off[3]
    loc_a = mm(phi[0], split(loc[1]), TN) + loc[0]
    loc_b = mm(phi[2], split(loc[3]), TN) + loc[2]
    whole = mm(second, first, NN)
    later = mm(second, split(off_a), NN) + off_b
    earlier = mm(first, split(loc_b), TN) + loc_a
    for to in range(out_ref.shape[0]):
        out_ref[to, 0] = whole
        out_ref[to, 1] = jnp.where(to > z, later, earlier)


def spread_kernel(at_ref, start_ref, end_ref, groups_ref, maps_ref, out_ref):
    z, x = at_ref[0], at_ref[1]
    count = groups_ref.shape[0]
    state, grad = start_ref[x], end_ref[x]
    for step in range(count - 1):
        back = count - 1 - step
        ahead = mm(split(groups_ref[step, 0]), split(state), NN) + groups_ref[step, 1]
        behind = mm(split(groups_ref[back, 0]), split(grad), TN) + groups_ref[back, 1]
        state = jnp.where(step < z, ahead, state)
        grad = jnp.where(back > z, behind, grad)
    for step in range(4):
        back = 3 - step
        out_ref[step, 0] = state
        out_ref[back, 1] = grad
        if step < 3:
            state = mm(split(maps_ref[step, 0]), split(state), NN) + maps_ref[step, 1]
            grad = mm(split(maps_ref[back, 0]), split(grad), TN) + maps_ref[back, 2]


def finish_kernel(
    ends_ref, maps_ref, q_ref, k_ref, v_ref, g_ref, inv_ref, ratio_ref, rk_ref, p_ref, w_ref,
    y_ref, du_ref, rows_ref, cols_ref, x_hbm,
    dq_ref, dk_ref, dv_ref, bound_ref, logit_ref, term_ref, x_ref, sem,
):
    fetch = pltpu.make_async_copy(x_hbm, x_ref, sem)
    fetch.start()
    heads = maps_ref.shape[0]
    hs = range(heads)
    row, lane = ids((T, T))
    strict = row > lane
    scale = 1.0 / math.sqrt(T)
    cols, rows = cols_ref[...], rows_ref[...]
    decay_cols, beta_cols, decay_rows, ends = [], [], [], []
    for h in hs:
        span = slice(h * T, (h + 1) * T)
        q, k, g = q_ref[:, span], k_ref[:, span], g_ref[:, span]
        qf, kf, vf = q.astype(F32), k.astype(F32), v_ref[:, span].astype(F32)
        beta = cols[:, h : h + 1]
        cum = cols[:, heads + h : heads + h + 1]
        norm_k = cols[:, 2 * heads + h : 2 * heads + h + 1]
        norm_q = cols[:, 3 * heads + h : 3 * heads + h + 1]
        norm_k_row = rows[2 * heads + h : 2 * heads + h + 1]
        end = rows[heads + h : heads + h + 1, T - 1 : T]
        grow, tail = jnp.exp(cum), jnp.exp(end - cum)
        m0, d = ends_ref[h, 0], ends_ref[h, 1]
        m_parts, d_parts = split(m0), split(d)
        u = w_ref[h] - mm(split(y_ref[h]), m_parts, NN)
        du = du_ref[h] + (tail * norm_k) * mm(k, d_parts, NN)
        u_parts = split(u)
        db = mm(split(inv_ref[h]), split(du), TN)
        db_parts = split(db)
        bound_ref[0, h] = mm(split(maps_ref[h, 0]), d_parts, TN) + maps_ref[h, 2]
        km = norm_k * mm(k, m_parts, NN)
        z = vf - grow * km
        dv_ref[:, span] = beta * db
        kn = norm_k * kf
        qn = (norm_q * scale) * qf
        dkn = -(beta * grow) * mm(db_parts, m_parts, NT)
        da = jnp.where(strict, -mm(db_parts, u_parts, NT), 0.0)
        ratio = ratio_ref[h]
        rka = da * rk_ref[h]
        hm = beta * ratio * da
        dkn = dkn + mm(split((hm + hm.T) * norm_k_row), k, NN)
        dp = mm(g, u_parts, NT)
        ds = ratio * dp
        dqn = mm(split(ds * norm_k_row), k, NN)
        dkn = dkn + mm(split(ds * (norm_q * scale)), q, TN)
        dom = mm(g, m_parts, NT)
        dqn = dqn + grow * dom
        dkt = tail * mm(u_parts, d_parts, NT)
        dkn = dkn + dkt
        both = beta * rka + dp * p_ref[h]
        tails = dkt * kn
        decay_cols.append(
            jnp.sum(both + grow * (dom * qn - beta * (db * km)) - tails, axis=1, keepdims=True)
        )
        beta_cols.append(jnp.sum(db * z + rka, axis=1, keepdims=True))
        decay_rows.append(jnp.sum(both, axis=0, keepdims=True))
        last = jnp.sum(
            jnp.sum(jnp.exp(end) * (d * m0) + tails, axis=0, keepdims=True), axis=1, keepdims=True
        )
        ends.append(jnp.broadcast_to(last, (1, T)))
        dot_q = jnp.sum(qf * dqn, axis=1, keepdims=True)
        dot_k = jnp.sum(kf * dkn, axis=1, keepdims=True)
        dq_ref[:, span] = (norm_q * scale) * (dqn - qf * (norm_q * norm_q * dot_q))
        dk_ref[:, span] = norm_k * (dkn - kf * (norm_k * norm_k * dot_k))
    turned = place(decay_cols + beta_cols, lane).T
    lane_one = lane[:heads]
    dcum = turned[:heads] - jnp.concatenate(decay_rows, axis=0)
    dcum = dcum + jnp.where(lane_one == T - 1, jnp.concatenate(ends, axis=0), 0.0)
    lower_ones = jnp.where(row >= lane, 1.0, 0.0).astype(BF16)
    ddecay = mm(split3(dcum), lower_ones, NN)
    beta_row = rows[:heads]
    dbeta = turned[heads : 2 * heads] * beta_row * (1.0 - beta_row)
    dshift = ddecay * rows[5 * heads : 6 * heads]
    logit = jnp.concatenate([dbeta, dshift], axis=0)
    logit_ref[...] = logit
    rate_sum = jnp.sum(ddecay * rows[4 * heads : 5 * heads], axis=1, keepdims=True)
    bias_sum = jnp.sum(dshift, axis=1, keepdims=True)
    param = jnp.broadcast_to(jnp.concatenate([rate_sum, bias_sum], axis=0), (2 * heads, T))
    high, low = split(logit)
    fetch.wait()
    pieces = term_ref.shape[0]
    width = x_ref.shape[1] // pieces
    for s in range(pieces):
        x = x_ref[:, s * width : (s + 1) * width]
        term_ref[s, :, :width] = lax.dot_general(
            high, x, NN, preferred_element_type=F32
        ) + lax.dot_general(low, x, NN, preferred_element_type=F32)
        term_ref[s, :, width:] = param


def window_kernel(at_ref, q_ref, g_ref, own_ref, near_ref, far_ref, dq_ref, stat_ref):
    kv_refs = (own_ref, near_ref, far_ref)
    z, x = at_ref[0], at_ref[1]
    row, lane = ids((T, T))
    gap = row - lane
    scale = 1.0 / math.sqrt(T)
    q, g = q_ref[...], g_ref[...]
    scores = []
    tiles = [(a, b) for a in range(4) for b in range(3)]
    for a, b in tiles:
        spread = gap + (jnp.where(x >= a, a, a - 4) + 4 * b) * T
        ok = (spread >= 0) & (spread < jnp.where(z >= b, WINDOW, 0))
        s = lax.dot_general(q, kv_refs[b][a, 0], NT, preferred_element_type=F32) * scale
        scores.append(jnp.where(ok, s, -1e30))
    top = scores[0]
    for s in scores[1:]:
        top = jnp.maximum(top, s)
    top = jnp.max(top, axis=1, keepdims=True)
    weights = [jnp.exp(s - top) for s in scores]
    total = weights[0]
    for w in weights[1:]:
        total = total + w
    total = 1.0 / jnp.sum(total, axis=1, keepdims=True)
    weights = [w * total for w in weights]
    slopes, terms = [], None
    for (a, b), w in zip(tiles, weights):
        slope = lax.dot_general(g, kv_refs[b][a, 1], NT, preferred_element_type=F32)
        slopes.append(slope)
        terms = w * slope if terms is None else terms + w * slope
    terms = jnp.sum(terms, axis=1, keepdims=True)
    stat_ref[...] = place([top, total, terms], lane).T[:8]
    dq = None
    for (a, b), w, slope in zip(tiles, weights, slopes):
        part = mm(split(w * (slope - terms) * scale), kv_refs[b][a, 0], NN)
        dq = part if dq is None else dq + part
    dq_ref[...] = dq


def key_kernel(
    at_ref, k_ref, v_ref, own_ref, near_ref, far_ref, own_stat, near_stat, far_stat, dk_ref, dv_ref
):
    qg_refs, stat_refs = (own_ref, near_ref, far_ref), (own_stat, near_stat, far_stat)
    z, x, count = at_ref[0], at_ref[1], at_ref[3]
    row, lane = ids((T, T))
    gap = lane - row
    scale = 1.0 / math.sqrt(T)
    k, v = k_ref[...], v_ref[...]
    dk, dv = jnp.zeros((T, T), F32), jnp.zeros((T, T), F32)
    for b in range(3):
        for a in range(4):
            spread = gap + (jnp.where(x >= a, -a, 4 - a) + 4 * b) * T
            ok = (spread >= 0) & (spread < jnp.where(z + b < count, WINDOW, 0))
            q, g, stat = qg_refs[b][a, 0], qg_refs[b][a, 1], stat_refs[b][a]
            s = lax.dot_general(k, q, NT, preferred_element_type=F32) * scale
            w = jnp.exp(jnp.where(ok, s - stat[0:1], -1e30)) * stat[1:2]
            slope = lax.dot_general(v, g, NT, preferred_element_type=F32)
            dv = dv + mm(split(w), g, NN)
            dk = dk + mm(split(w * (slope - stat[2:3]) * scale), q, NN)
    dk_ref[...] = dk
    dv_ref[...] = dv


def input_kernel(*refs):
    count = (len(refs) - 3) // 2
    row_refs, chunk_refs = refs[:count], refs[count : 2 * count]
    out_ref, rows_ref, w_ref = refs[2 * count :]
    for d in range(count):
        rows_ref[8 * d : 8 * d + 8, :] = row_refs[d][...]
        w_ref[8 * d : 8 * d + 8, :] = chunk_refs[d][...].astype(F32)
    high, low = split(rows_ref[...])
    w = w_ref[...].astype(BF16)
    out_ref[...] = lax.dot_general(high, w, TN, preferred_element_type=F32) + lax.dot_general(
        low, w, TN, preferred_element_type=F32
    )


VM = pl.BlockSpec(memory_space=pltpu.VMEM)
SM = pl.BlockSpec(memory_space=pltpu.SMEM)
ANY = pl.BlockSpec(memory_space=pl.ANY)


def f32(*shape):
    return jax.ShapeDtypeStruct(shape, F32)


def call(kernel, outs, specs, *args, flops=10**8, scratch=(), limit=24 * 2**20):
    return run(kernel, outs, specs, args, flops, scratch, limit)


def exchange(value, axis):
    return lax.all_to_all(value, axis, split_axis=0, concat_axis=0, tiled=True)


def run(kernel, outs, specs, args, flops, scratch, limit):
    return pl.pallas_call(
        kernel,
        out_shape=outs,
        in_specs=specs,
        out_specs=jax.tree.map(lambda _: VM, outs),
        scratch_shapes=scratch,
        cost_estimate=pl.CostEstimate(flops=flops, bytes_accessed=4 * 10**6, transcendentals=0),
        compiler_params=pltpu.CompilerParams(vmem_limit_bytes=limit),
    )(*args)


WHOLE = 60 * 1024 * 1024


def up_by(value, by, count):
    pairs = [(i, i + by) for i in range(count) if 0 <= i + by < count]
    return lax.ppermute(value, "seq_0", pairs)


def turn(value, axis, by, count):
    return lax.ppermute(value, axis, [(i, (i + by) % count) for i in range(count)])


def shards(
    layer_input, beta_weight, decay_weight, log_rate, decay_bias, delta_query, delta_key,
    delta_value, delta_out_grad, state_init, state_grad_next, attn_query, attn_key, attn_value,
    attn_out_grad,
):
    z_count, x_count = lax.axis_size("seq_0"), lax.axis_size("seq_1")
    head_count = lax.axis_size("head")
    heads = beta_weight.shape[0]
    width = layer_input.shape[1]
    pieces = z_count * x_count
    at = jnp.stack(
        [lax.axis_index("seq_0"), lax.axis_index("seq_1"), lax.axis_index("head"), z_count]
    ).astype(jnp.int32)
    others = range(1, x_count)

    mine = jnp.stack([attn_key, attn_value, attn_query, attn_out_grad])
    line = [mine] + [turn(mine, "seq_1", d, x_count) for d in others]

    bf16_chunk = jax.ShapeDtypeStruct((2 * heads, width // head_count), BF16)
    maps, inv, ratio, rk, p, w, y, du, rows, cols, *chunks = call(
        prepare_kernel,
        (f32(heads, 3, T, T),) + (f32(heads, T, T),) * 7 + (f32(6 * heads, T), f32(T, T))
        + (bf16_chunk,) * head_count,
        [SM, ANY, VM, VM, SM, SM, VM, VM, VM, VM],
        at, layer_input, beta_weight, decay_weight, log_rate, decay_bias, delta_query, delta_key,
        delta_value, delta_out_grad,
        scratch=[
            pltpu.VMEM((2 * heads, width), BF16), pltpu.VMEM((T, width), BF16),
            pltpu.SemaphoreType.DMA,
        ],
        limit=WHOLE,
    )
    blocks = exchange(maps, "seq_1")
    kv, qg = jnp.stack([a[:2] for a in line]), jnp.stack([a[2:] for a in line])
    kv_all = [kv] + [up_by(kv, d, z_count) for d in (1, 2)]
    qg_all = [qg] + [up_by(qg, -d, z_count) for d in (1, 2)]
    groups = call(group_kernel, f32(z_count, 2, T, T), [SM, VM], at, blocks)

    groups = exchange(groups, "seq_0")
    dq_attn, stat = call(
        window_kernel,
        (f32(T, T), f32(8, T)),
        [SM] + [VM] * 5,
        at, attn_query, attn_out_grad, *kv_all,
    )
    stat = jnp.stack([stat] + [turn(stat, "seq_1", d, x_count) for d in others])
    stat_all = [stat] + [up_by(stat, -d, z_count) for d in (1, 2)]
    dk_attn, dv_attn = call(
        key_kernel,
        (f32(T, T), f32(T, T)),
        [SM] + [VM] * 8,
        at, attn_key, attn_value, *qg_all, *stat_all,
    )
    chunks = [chunks[0]] + [turn(chunks[d], "head", d, head_count) for d in range(1, head_count)]

    ends = call(
        spread_kernel,
        f32(x_count, 2, T, T),
        [SM] + [VM] * 4,
        at, state_init, state_grad_next, groups, blocks,
    )
    ends = exchange(ends, "seq_1")

    dq, dk, dv, bound, logit, terms = call(
        finish_kernel,
        (f32(T, heads * T),) * 3
        + (f32(1, heads, T, T), f32(2 * heads, T), f32(pieces, 2 * heads, width // pieces + T)),
        [VM] * 15 + [ANY],
        ends, maps, delta_query, delta_key, delta_value, delta_out_grad, inv, ratio, rk, p, w, y,
        du, rows, cols, layer_input,
        scratch=[pltpu.VMEM((T, width), BF16), pltpu.SemaphoreType.DMA],
        limit=WHOLE,
    )
    terms = exchange(terms, SEQ)
    every = [logit] + [turn(logit, "head", d, head_count) for d in range(1, head_count)]
    input_grad = call(
        input_kernel,
        f32(T, width // head_count),
        [VM] * (2 * head_count),
        *every, *chunks,
        scratch=[
            pltpu.VMEM((2 * heads * head_count, T), F32),
            pltpu.VMEM((2 * heads * head_count, width // head_count), F32),
        ],
    )
    terms = jnp.sum(terms, axis=0)
    part = width // pieces
    return (
        dq, dk, dv, bound, input_grad,
        terms[:heads, :part], terms[heads:, :part],
        terms[:heads, part], terms[heads:, part],
        dq_attn, dk_attn, dv_attn,
    )


def solution(mesh):
    torus = Mesh(mesh.devices.reshape(8, 4, mesh.shape["head"]), ("seq_0", "seq_1", "head"))
    tokens, by_head = P(SEQ, "head"), P("head", None, None)
    in_specs = (
        P(SEQ, None), P("head", None), P("head", None), P("head"), P("head"),
        tokens, tokens, tokens, tokens, by_head, by_head, tokens, tokens, tokens, tokens,
    )
    out_specs = (
        tokens, tokens, tokens, P(SEQ, "head", None, None), tokens,
        P("head", SEQ), P("head", SEQ), P("head"), P("head"), tokens, tokens, tokens,
    )

    return jax.shard_map(
        shards, mesh=torus, in_specs=in_specs, out_specs=out_specs, check_vma=False
    )
```

```python
import math

import jax
import jax.numpy as jnp
from jax import lax
from jax.experimental import pallas as pl
from jax.experimental.pallas import tpu as pltpu
from jax.sharding import Mesh
from jax.sharding import PartitionSpec as P


WINDOW = 1024
T = 128
SEQ = ("seq_0", "seq_1")
F32 = jnp.float32
BF16 = jnp.bfloat16
NN = (((1,), (0,)), ((), ()))
NT = (((1,), (1,)), ((), ()))
TN = (((0,), (0,)), ((), ()))


def split(value):
    high = value.astype(BF16)
    return high, (value - high.astype(F32)).astype(BF16)


def split3(value):
    high = value.astype(BF16)
    rest = value - high.astype(F32)
    mid = rest.astype(BF16)
    return high, mid, (rest - mid.astype(F32)).astype(BF16)


def mm(left, right, dims):
    lefts = left if isinstance(left, tuple) else (left,)
    rights = right if isinstance(right, tuple) else (right,)
    total = None
    for i, a in enumerate(lefts):
        for j, b in enumerate(rights):
            if i + j < max(len(lefts), len(rights)):
                term = lax.dot_general(a, b, dims, preferred_element_type=F32)
                total = term if total is None else total + term
    return total


def ids(shape):
    return (
        lax.broadcasted_iota(jnp.int32, shape, 0),
        lax.broadcasted_iota(jnp.int32, shape, 1),
    )


def place(columns, lane):
    result = jnp.zeros((T, T), F32)
    for at, column in enumerate(columns):
        result = jnp.where(lane == at, column, result)
    return result


def prepare_kernel(
    x_hbm, wb_ref, wd_ref, rate_ref, bias_ref, q_ref, k_ref, v_ref, g_ref,
    maps_ref, inv_ref, ratio_ref, rk_ref, p_ref, w_out_ref, y_ref, du_ref, rows_ref, cols_ref,
    *rest,
):
    chunk_refs, (w_ref, x_ref, sem) = rest[:-3], rest[-3:]
    fetch = pltpu.make_async_copy(x_hbm, x_ref, sem)
    fetch.start()
    heads = maps_ref.shape[0]
    w_ref[...] = jnp.concatenate(
        [wb_ref[...].astype(F32), wd_ref[...].astype(F32)], axis=0
    ).astype(BF16)
    count = len(chunk_refs)
    size = w_ref.shape[1] // count
    for d, chunk_ref in enumerate(chunk_refs):
        to = lax.axis_index("head") + d
        to = jnp.where(to >= count, to - count, to)
        chunk_ref[...] = w_ref[:, pl.ds(pl.multiple_of(to * size, size), size)]
    row, lane = ids((T, T))
    lower, strict = row >= lane, row > lane
    eye = jnp.where(row == lane, 1.0, 0.0)
    hs = range(heads)
    span = [slice(h * T, (h + 1) * T) for h in hs]
    k = [k_ref[:, span[h]] for h in hs]
    q = [q_ref[:, span[h]] for h in hs]
    v = [v_ref[:, span[h]] for h in hs]
    g = [g_ref[:, span[h]] for h in hs]
    norm_k, norm_q = [], []
    for h in hs:
        kf, qf = k[h].astype(F32), q[h].astype(F32)
        norm_k.append(lax.rsqrt(jnp.sum(kf * kf, axis=1, keepdims=True) + 1e-6))
        norm_q.append(lax.rsqrt(jnp.sum(qf * qf, axis=1, keepdims=True) + 1e-6))
    norm_rows = place(norm_k + norm_q, lane).T
    norm_k_row = norm_rows[:heads]
    norm_q_row = norm_rows[heads : 2 * heads]
    for h in hs:
        rk_ref[h] = mm(k[h], k[h], NT) * norm_k[h] * norm_k_row[h : h + 1]
        p_ref[h] = mm(q[h], k[h], NT) * (norm_q[h] * (1.0 / math.sqrt(T))) * norm_k_row[h : h + 1]
    rates = jnp.concatenate([jnp.full((1, T), rate_ref[h], F32) for h in hs], axis=0)
    biases = jnp.concatenate([jnp.full((1, T), bias_ref[h], F32) for h in hs], axis=0)
    fetch.wait()
    logits = lax.dot_general(w_ref[...], x_ref[...], NT, preferred_element_type=F32)
    beta_row = jax.nn.sigmoid(logits[:heads])
    shifted = logits[heads:] + biases
    soft = jnp.maximum(shifted, 0.0) + jnp.log1p(jnp.exp(-jnp.abs(shifted)))
    decay_row = -jnp.exp(rates) * soft
    upper_ones = jnp.where(row <= lane, 1.0, 0.0).astype(BF16)
    cum_row = mm(split3(decay_row), upper_ones, NN)
    gate_slope = -jnp.exp(rates) * jax.nn.sigmoid(shifted)
    turned = jnp.concatenate([beta_row, cum_row, jnp.zeros((T - 2 * heads, T), F32)], axis=0).T
    beta_c = [turned[:, h : h + 1] for h in hs]
    cum_c = [turned[:, heads + h : heads + h + 1] for h in hs]
    last = cum_row[:, T - 1 : T]
    rows_ref[...] = jnp.concatenate(
        [beta_row, cum_row, norm_k_row, norm_q_row, decay_row, gate_slope], axis=0
    )
    cols_ref[...] = place(beta_c + cum_c + norm_k + norm_q, lane)
    scale = 1.0 / math.sqrt(T)
    ratio, solve, low = [], [], []
    for h in hs:
        r = jnp.where(
            lower, jnp.exp(jnp.where(lower, cum_c[h] - cum_row[h : h + 1], 0.0)), 0.0
        )
        ratio.append(r)
        ratio_ref[h] = r
        rk = jnp.where(strict, r * rk_ref[h], 0.0)
        rk_ref[h] = rk
        low.append(rk * beta_c[h])
    for h in hs:
        same = (row // 2) == (lane // 2)
        solve.append(jnp.where(same, -low[h], 0.0) + eye)
    size = 2
    while size < T:
        block = (row // (2 * size) == lane // (2 * size)) & (row // size != lane // size)
        parts = [split(s) for s in solve]
        corner = [split(jnp.where(block, low[h], 0.0)) for h in hs]
        inner = [split(mm(corner[h], parts[h], NN)) for h in hs]
        solve = [solve[h] - mm(parts[h], inner[h], NN) for h in hs]
        size *= 2
    for h in hs:
        inv_ref[h] = solve[h]
        grow_c, grow_row = jnp.exp(cum_c[h]), jnp.exp(cum_row[h : h + 1])
        end = last[h : h + 1]
        tail_c = jnp.exp(end - cum_c[h])
        bv = beta_row[h : h + 1]
        w = mm(split(solve[h] * bv), v[h], NN)
        y = mm(split(solve[h] * (bv * grow_row * norm_k_row[h : h + 1])), k[h], NN)
        w_out_ref[h] = w
        y_ref[h] = y
        p = ratio[h] * p_ref[h]
        p_ref[h] = p
        du = mm(split(p), g[h], TN)
        du_ref[h] = du
        out_scale = tail_c * norm_k[h]
        maps_ref[h, 0] = jnp.exp(end) * eye - mm(k[h], split(out_scale * y), TN)
        maps_ref[h, 1] = mm(k[h], split(out_scale * w), TN)
        own = mm(q[h], split((grow_c * norm_q[h] * scale) * g[h].astype(F32)), TN)
        maps_ref[h, 2] = own - mm(split(y), split(du), TN)


def group_kernel(maps_ref, out_ref):
    z = lax.axis_index("seq_0")
    phi = [split(maps_ref[x, 0]) for x in range(4)]
    off = [maps_ref[x, 1] for x in range(4)]
    loc = [maps_ref[x, 2] for x in range(4)]
    first = split(mm(phi[1], phi[0], NN))
    second = split(mm(phi[3], phi[2], NN))
    off_a = mm(phi[1], split(off[0]), NN) + off[1]
    off_b = mm(phi[3], split(off[2]), NN) + off[3]
    loc_a = mm(phi[0], split(loc[1]), TN) + loc[0]
    loc_b = mm(phi[2], split(loc[3]), TN) + loc[2]
    whole = mm(second, first, NN)
    later = mm(second, split(off_a), NN) + off_b
    earlier = mm(first, split(loc_b), TN) + loc_a
    for to in range(out_ref.shape[0]):
        out_ref[to, 0] = whole
        out_ref[to, 1] = jnp.where(to > z, later, earlier)


def spread_kernel(start_ref, end_ref, groups_ref, maps_ref, out_ref):
    z, x = lax.axis_index("seq_0"), lax.axis_index("seq_1")
    count = groups_ref.shape[0]
    state, grad = start_ref[x], end_ref[x]
    for step in range(count - 1):
        back = count - 1 - step
        ahead = mm(split(groups_ref[step, 0]), split(state), NN) + groups_ref[step, 1]
        behind = mm(split(groups_ref[back, 0]), split(grad), TN) + groups_ref[back, 1]
        state = jnp.where(step < z, ahead, state)
        grad = jnp.where(back > z, behind, grad)
    for step in range(4):
        back = 3 - step
        out_ref[step, 0] = state
        out_ref[back, 1] = grad
        if step < 3:
            state = mm(split(maps_ref[step, 0]), split(state), NN) + maps_ref[step, 1]
            grad = mm(split(maps_ref[back, 0]), split(grad), TN) + maps_ref[back, 2]


def finish_kernel(
    ends_ref, maps_ref, q_ref, k_ref, v_ref, g_ref, inv_ref, ratio_ref, rk_ref, p_ref, w_ref,
    y_ref, du_ref, rows_ref, cols_ref, x_hbm,
    dq_ref, dk_ref, dv_ref, bound_ref, logit_ref, term_ref, x_ref, sem,
):
    fetch = pltpu.make_async_copy(x_hbm, x_ref, sem)
    fetch.start()
    heads = maps_ref.shape[0]
    hs = range(heads)
    row, lane = ids((T, T))
    strict = row > lane
    scale = 1.0 / math.sqrt(T)
    cols, rows = cols_ref[...], rows_ref[...]
    decay_cols, beta_cols, decay_rows, ends = [], [], [], []
    for h in hs:
        span = slice(h * T, (h + 1) * T)
        q, k, g = q_ref[:, span], k_ref[:, span], g_ref[:, span]
        qf, kf, vf = q.astype(F32), k.astype(F32), v_ref[:, span].astype(F32)
        beta = cols[:, h : h + 1]
        cum = cols[:, heads + h : heads + h + 1]
        norm_k = cols[:, 2 * heads + h : 2 * heads + h + 1]
        norm_q = cols[:, 3 * heads + h : 3 * heads + h + 1]
        norm_k_row = rows[2 * heads + h : 2 * heads + h + 1]
        end = rows[heads + h : heads + h + 1, T - 1 : T]
        grow, tail = jnp.exp(cum), jnp.exp(end - cum)
        m0, d = ends_ref[h, 0], ends_ref[h, 1]
        m_parts, d_parts = split(m0), split(d)
        u = w_ref[h] - mm(split(y_ref[h]), m_parts, NN)
        du = du_ref[h] + (tail * norm_k) * mm(k, d_parts, NN)
        u_parts = split(u)
        db = mm(split(inv_ref[h]), split(du), TN)
        db_parts = split(db)
        bound_ref[0, h] = mm(split(maps_ref[h, 0]), d_parts, TN) + maps_ref[h, 2]
        km = norm_k * mm(k, m_parts, NN)
        z = vf - grow * km
        dv_ref[:, span] = beta * db
        kn = norm_k * kf
        qn = (norm_q * scale) * qf
        dkn = -(beta * grow) * mm(db_parts, m_parts, NT)
        da = jnp.where(strict, -mm(db_parts, u_parts, NT), 0.0)
        ratio = ratio_ref[h]
        rka = da * rk_ref[h]
        hm = beta * ratio * da
        dkn = dkn + mm(split((hm + hm.T) * norm_k_row), k, NN)
        dp = mm(g, u_parts, NT)
        ds = ratio * dp
        dqn = mm(split(ds * norm_k_row), k, NN)
        dkn = dkn + mm(split(ds * (norm_q * scale)), q, TN)
        dom = mm(g, m_parts, NT)
        dqn = dqn + grow * dom
        dkt = tail * mm(u_parts, d_parts, NT)
        dkn = dkn + dkt
        both = beta * rka + dp * p_ref[h]
        tails = dkt * kn
        decay_cols.append(
            jnp.sum(both + grow * (dom * qn - beta * (db * km)) - tails, axis=1, keepdims=True)
        )
        beta_cols.append(jnp.sum(db * z + rka, axis=1, keepdims=True))
        decay_rows.append(jnp.sum(both, axis=0, keepdims=True))
        last = jnp.sum(
            jnp.sum(jnp.exp(end) * (d * m0) + tails, axis=0, keepdims=True), axis=1, keepdims=True
        )
        ends.append(jnp.broadcast_to(last, (1, T)))
        dot_q = jnp.sum(qf * dqn, axis=1, keepdims=True)
        dot_k = jnp.sum(kf * dkn, axis=1, keepdims=True)
        dq_ref[:, span] = (norm_q * scale) * (dqn - qf * (norm_q * norm_q * dot_q))
        dk_ref[:, span] = norm_k * (dkn - kf * (norm_k * norm_k * dot_k))
    turned = place(decay_cols + beta_cols, lane).T
    lane_one = lane[:heads]
    dcum = turned[:heads] - jnp.concatenate(decay_rows, axis=0)
    dcum = dcum + jnp.where(lane_one == T - 1, jnp.concatenate(ends, axis=0), 0.0)
    lower_ones = jnp.where(row >= lane, 1.0, 0.0).astype(BF16)
    ddecay = mm(split3(dcum), lower_ones, NN)
    beta_row = rows[:heads]
    dbeta = turned[heads : 2 * heads] * beta_row * (1.0 - beta_row)
    dshift = ddecay * rows[5 * heads : 6 * heads]
    logit = jnp.concatenate([dbeta, dshift], axis=0)
    logit_ref[...] = logit
    rate_sum = jnp.sum(ddecay * rows[4 * heads : 5 * heads], axis=1, keepdims=True)
    bias_sum = jnp.sum(dshift, axis=1, keepdims=True)
    param = jnp.broadcast_to(jnp.concatenate([rate_sum, bias_sum], axis=0), (2 * heads, T))
    high, low = split(logit)
    fetch.wait()
    pieces = term_ref.shape[0]
    width = x_ref.shape[1] // pieces
    for s in range(pieces):
        x = x_ref[:, s * width : (s + 1) * width]
        term_ref[s, :, :width] = lax.dot_general(
            high, x, NN, preferred_element_type=F32
        ) + lax.dot_general(low, x, NN, preferred_element_type=F32)
        term_ref[s, :, width:] = param


def window_kernel(q_ref, g_ref, own_ref, near_ref, far_ref, dq_ref, stat_ref):
    kv_refs = (own_ref, near_ref, far_ref)
    z, x = lax.axis_index("seq_0"), lax.axis_index("seq_1")
    row, lane = ids((T, T))
    gap = row - lane
    scale = 1.0 / math.sqrt(T)
    q, g = q_ref[...], g_ref[...]
    scores = []
    tiles = [(a, b) for a in range(4) for b in range(3)]
    for a, b in tiles:
        spread = gap + (jnp.where(x >= a, a, a - 4) + 4 * b) * T
        ok = (spread >= 0) & (spread < jnp.where(z >= b, WINDOW, 0))
        s = lax.dot_general(q, kv_refs[b][a, 0], NT, preferred_element_type=F32) * scale
        scores.append(jnp.where(ok, s, -1e30))
    top = scores[0]
    for s in scores[1:]:
        top = jnp.maximum(top, s)
    top = jnp.max(top, axis=1, keepdims=True)
    weights = [jnp.exp(s - top) for s in scores]
    total = weights[0]
    for w in weights[1:]:
        total = total + w
    total = 1.0 / jnp.sum(total, axis=1, keepdims=True)
    weights = [w * total for w in weights]
    slopes, terms = [], None
    for (a, b), w in zip(tiles, weights):
        slope = lax.dot_general(g, kv_refs[b][a, 1], NT, preferred_element_type=F32)
        slopes.append(slope)
        terms = w * slope if terms is None else terms + w * slope
    terms = jnp.sum(terms, axis=1, keepdims=True)
    stat_ref[...] = place([top, total, terms], lane).T[:8]
    dq = None
    for (a, b), w, slope in zip(tiles, weights, slopes):
        part = mm(split(w * (slope - terms) * scale), kv_refs[b][a, 0], NN)
        dq = part if dq is None else dq + part
    dq_ref[...] = dq


def key_kernel(
    k_ref, v_ref, own_ref, near_ref, far_ref, own_stat, near_stat, far_stat, dk_ref, dv_ref
):
    qg_refs, stat_refs = (own_ref, near_ref, far_ref), (own_stat, near_stat, far_stat)
    z, x = lax.axis_index("seq_0"), lax.axis_index("seq_1")
    count = lax.axis_size("seq_0")
    row, lane = ids((T, T))
    gap = lane - row
    scale = 1.0 / math.sqrt(T)
    k, v = k_ref[...], v_ref[...]
    dk, dv = jnp.zeros((T, T), F32), jnp.zeros((T, T), F32)
    for b in range(3):
        for a in range(4):
            spread = gap + (jnp.where(x >= a, -a, 4 - a) + 4 * b) * T
            ok = (spread >= 0) & (spread < jnp.where(z + b < count, WINDOW, 0))
            q, g, stat = qg_refs[b][a, 0], qg_refs[b][a, 1], stat_refs[b][a]
            s = lax.dot_general(k, q, NT, preferred_element_type=F32) * scale
            w = jnp.exp(jnp.where(ok, s - stat[0:1], -1e30)) * stat[1:2]
            slope = lax.dot_general(v, g, NT, preferred_element_type=F32)
            dv = dv + mm(split(w), g, NN)
            dk = dk + mm(split(w * (slope - stat[2:3]) * scale), q, NN)
    dk_ref[...] = dk
    dv_ref[...] = dv


def input_kernel(*refs):
    count = (len(refs) - 3) // 2
    row_refs, chunk_refs = refs[:count], refs[count : 2 * count]
    out_ref, rows_ref, w_ref = refs[2 * count :]
    for d in range(count):
        rows_ref[8 * d : 8 * d + 8, :] = row_refs[d][...]
        w_ref[8 * d : 8 * d + 8, :] = chunk_refs[d][...].astype(F32)
    high, low = split(rows_ref[...])
    w = w_ref[...].astype(BF16)
    out_ref[...] = lax.dot_general(high, w, TN, preferred_element_type=F32) + lax.dot_general(
        low, w, TN, preferred_element_type=F32
    )


VM = pl.BlockSpec(memory_space=pltpu.VMEM)
SM = pl.BlockSpec(memory_space=pltpu.SMEM)
ANY = pl.BlockSpec(memory_space=pl.ANY)


def f32(*shape):
    return jax.ShapeDtypeStruct(shape, F32)


def call(kernel, outs, specs, *args, flops=10**8, scratch=(), limit=24 * 2**20):
    return run(kernel, outs, specs, args, flops, scratch, limit)


def exchange(value, axis):
    return lax.all_to_all(value, axis, split_axis=0, concat_axis=0, tiled=True)


def run(kernel, outs, specs, args, flops, scratch, limit):
    return pl.pallas_call(
        kernel,
        out_shape=outs,
        in_specs=specs,
        out_specs=jax.tree.map(lambda _: VM, outs),
        scratch_shapes=scratch,
        cost_estimate=pl.CostEstimate(flops=flops, bytes_accessed=4 * 10**6, transcendentals=0),
        compiler_params=pltpu.CompilerParams(vmem_limit_bytes=limit),
    )(*args)


WHOLE = 60 * 1024 * 1024


def up_by(value, by, count):
    pairs = [(i, i + by) for i in range(count) if 0 <= i + by < count]
    return lax.ppermute(value, "seq_0", pairs)


def turn(value, axis, by, count):
    return lax.ppermute(value, axis, [(i, (i + by) % count) for i in range(count)])


def shards(
    layer_input, beta_weight, decay_weight, log_rate, decay_bias, delta_query, delta_key,
    delta_value, delta_out_grad, state_init, state_grad_next, attn_query, attn_key, attn_value,
    attn_out_grad,
):
    z_count, x_count = lax.axis_size("seq_0"), lax.axis_size("seq_1")
    head_count = lax.axis_size("head")
    heads = beta_weight.shape[0]
    width = layer_input.shape[1]
    pieces = z_count * x_count
    others = range(1, x_count)

    mine = jnp.stack([attn_key, attn_value, attn_query, attn_out_grad])
    line = [mine] + [turn(mine, "seq_1", d, x_count) for d in others]

    bf16_chunk = jax.ShapeDtypeStruct((2 * heads, width // head_count), BF16)
    maps, inv, ratio, rk, p, w, y, du, rows, cols, *chunks = call(
        prepare_kernel,
        (f32(heads, 3, T, T),) + (f32(heads, T, T),) * 7 + (f32(6 * heads, T), f32(T, T))
        + (bf16_chunk,) * head_count,
        [ANY, VM, VM, SM, SM, VM, VM, VM, VM],
        layer_input, beta_weight, decay_weight, log_rate, decay_bias, delta_query, delta_key,
        delta_value, delta_out_grad,
        scratch=[
            pltpu.VMEM((2 * heads, width), BF16), pltpu.VMEM((T, width), BF16),
            pltpu.SemaphoreType.DMA,
        ],
        limit=WHOLE,
    )
    blocks = exchange(maps, "seq_1")
    kv, qg = jnp.stack([a[:2] for a in line]), jnp.stack([a[2:] for a in line])
    kv_all = [kv] + [up_by(kv, d, z_count) for d in (1, 2)]
    qg_all = [qg] + [up_by(qg, -d, z_count) for d in (1, 2)]
    groups = call(group_kernel, f32(z_count, 2, T, T), [VM], blocks)

    groups = exchange(groups, "seq_0")
    dq_attn, stat = call(
        window_kernel,
        (f32(T, T), f32(8, T)),
        [VM] * 5,
        attn_query, attn_out_grad, *kv_all,
    )
    stat = jnp.stack([stat] + [turn(stat, "seq_1", d, x_count) for d in others])
    stat_all = [stat] + [up_by(stat, -d, z_count) for d in (1, 2)]
    dk_attn, dv_attn = call(
        key_kernel,
        (f32(T, T), f32(T, T)),
        [VM] * 8,
        attn_key, attn_value, *qg_all, *stat_all,
    )
    chunks = [chunks[0]] + [turn(chunks[d], "head", d, head_count) for d in range(1, head_count)]

    ends = call(
        spread_kernel,
        f32(x_count, 2, T, T),
        [VM] * 4,
        state_init, state_grad_next, groups, blocks,
    )
    ends = exchange(ends, "seq_1")

    dq, dk, dv, bound, logit, terms = call(
        finish_kernel,
        (f32(T, heads * T),) * 3
        + (f32(1, heads, T, T), f32(2 * heads, T), f32(pieces, 2 * heads, width // pieces + T)),
        [VM] * 15 + [ANY],
        ends, maps, delta_query, delta_key, delta_value, delta_out_grad, inv, ratio, rk, p, w, y,
        du, rows, cols, layer_input,
        scratch=[pltpu.VMEM((T, width), BF16), pltpu.SemaphoreType.DMA],
        limit=WHOLE,
    )
    terms = exchange(terms, SEQ)
    every = [logit] + [turn(logit, "head", d, head_count) for d in range(1, head_count)]
    input_grad = call(
        input_kernel,
        f32(T, width // head_count),
        [VM] * (2 * head_count),
        *every, *chunks,
        scratch=[
            pltpu.VMEM((2 * heads * head_count, T), F32),
            pltpu.VMEM((2 * heads * head_count, width // head_count), F32),
        ],
    )
    terms = jnp.sum(terms, axis=0)
    part = width // pieces
    return (
        dq, dk, dv, bound, input_grad,
        terms[:heads, :part], terms[heads:, :part],
        terms[:heads, part], terms[heads:, part],
        dq_attn, dk_attn, dv_attn,
    )


def solution(mesh):
    torus = Mesh(mesh.devices.reshape(8, 4, mesh.shape["head"]), ("seq_0", "seq_1", "head"))
    tokens, by_head = P(SEQ, "head"), P("head", None, None)
    in_specs = (
        P(SEQ, None), P("head", None), P("head", None), P("head"), P("head"),
        tokens, tokens, tokens, tokens, by_head, by_head, tokens, tokens, tokens, tokens,
    )
    out_specs = (
        tokens, tokens, tokens, P(SEQ, "head", None, None), tokens,
        P("head", SEQ), P("head", SEQ), P("head"), P("head"), tokens, tokens, tokens,
    )

    return jax.shard_map(
        shards, mesh=torus, in_specs=in_specs, out_specs=out_specs, check_vma=False
    )
```

```python
import math

import jax
import jax.numpy as jnp
from jax import lax
from jax.experimental import pallas as pl
from jax.experimental.pallas import tpu as pltpu
from jax.sharding import Mesh
from jax.sharding import PartitionSpec as P


WINDOW = 1024
T = 128
SEQ = ("seq_0", "seq_1")
F32 = jnp.float32
BF16 = jnp.bfloat16
NN = (((1,), (0,)), ((), ()))
NT = (((1,), (1,)), ((), ()))
TN = (((0,), (0,)), ((), ()))


def split(value):
    high = value.astype(BF16)
    return high, (value - high.astype(F32)).astype(BF16)


def split3(value):
    high = value.astype(BF16)
    rest = value - high.astype(F32)
    mid = rest.astype(BF16)
    return high, mid, (rest - mid.astype(F32)).astype(BF16)


def mm(left, right, dims):
    lefts = left if isinstance(left, tuple) else (left,)
    rights = right if isinstance(right, tuple) else (right,)
    total = None
    for i, a in enumerate(lefts):
        for j, b in enumerate(rights):
            if i + j < max(len(lefts), len(rights)):
                term = lax.dot_general(a, b, dims, preferred_element_type=F32)
                total = term if total is None else total + term
    return total


def ids(shape):
    return (
        lax.broadcasted_iota(jnp.int32, shape, 0),
        lax.broadcasted_iota(jnp.int32, shape, 1),
    )


def place(columns, lane):
    result = jnp.zeros((T, T), F32)
    for at, column in enumerate(columns):
        result = jnp.where(lane == at, column, result)
    return result


def prepare_kernel(
    x_hbm, wb_ref, wd_ref, rate_ref, bias_ref, q_ref, k_ref, v_ref, g_ref,
    maps_ref, inv_ref, ratio_ref, rk_ref, p_ref, w_out_ref, y_ref, du_ref, rows_ref, cols_ref,
    *rest,
):
    chunk_refs, (w_ref, x_ref, sem) = rest[:-3], rest[-3:]
    fetch = pltpu.make_async_copy(x_hbm, x_ref, sem)
    fetch.start()
    heads = maps_ref.shape[0]
    w_ref[...] = jnp.concatenate(
        [wb_ref[...].astype(F32), wd_ref[...].astype(F32)], axis=0
    ).astype(BF16)
    half = chunk_refs[0].shape[0]
    size = chunk_refs[0].shape[2]
    for d in range(2 * half):
        to = lax.axis_index("head") ^ d
        chunk_refs[d // half][d % half] = w_ref[:, pl.ds(pl.multiple_of(to * size, size), size)]
    row, lane = ids((T, T))
    lower, strict = row >= lane, row > lane
    eye = jnp.where(row == lane, 1.0, 0.0)
    hs = range(heads)
    span = [slice(h * T, (h + 1) * T) for h in hs]
    k = [k_ref[:, span[h]] for h in hs]
    q = [q_ref[:, span[h]] for h in hs]
    v = [v_ref[:, span[h]] for h in hs]
    g = [g_ref[:, span[h]] for h in hs]
    norm_k, norm_q = [], []
    for h in hs:
        kf, qf = k[h].astype(F32), q[h].astype(F32)
        norm_k.append(lax.rsqrt(jnp.sum(kf * kf, axis=1, keepdims=True) + 1e-6))
        norm_q.append(lax.rsqrt(jnp.sum(qf * qf, axis=1, keepdims=True) + 1e-6))
    norm_rows = place(norm_k + norm_q, lane).T
    norm_k_row = norm_rows[:heads]
    norm_q_row = norm_rows[heads : 2 * heads]
    for h in hs:
        rk_ref[h] = mm(k[h], k[h], NT) * norm_k[h] * norm_k_row[h : h + 1]
        p_ref[h] = mm(q[h], k[h], NT) * (norm_q[h] * (1.0 / math.sqrt(T))) * norm_k_row[h : h + 1]
    rates = jnp.concatenate([jnp.full((1, T), rate_ref[h], F32) for h in hs], axis=0)
    biases = jnp.concatenate([jnp.full((1, T), bias_ref[h], F32) for h in hs], axis=0)
    fetch.wait()
    logits = lax.dot_general(w_ref[...], x_ref[...], NT, preferred_element_type=F32)
    beta_row = jax.nn.sigmoid(logits[:heads])
    shifted = logits[heads:] + biases
    soft = jnp.maximum(shifted, 0.0) + jnp.log1p(jnp.exp(-jnp.abs(shifted)))
    decay_row = -jnp.exp(rates) * soft
    upper_ones = jnp.where(row <= lane, 1.0, 0.0).astype(BF16)
    cum_row = mm(split3(decay_row), upper_ones, NN)
    gate_slope = -jnp.exp(rates) * jax.nn.sigmoid(shifted)
    turned = jnp.concatenate([beta_row, cum_row, jnp.zeros((T - 2 * heads, T), F32)], axis=0).T
    beta_c = [turned[:, h : h + 1] for h in hs]
    cum_c = [turned[:, heads + h : heads + h + 1] for h in hs]
    last = cum_row[:, T - 1 : T]
    rows_ref[...] = jnp.concatenate(
        [beta_row, cum_row, norm_k_row, norm_q_row, decay_row, gate_slope], axis=0
    )
    cols_ref[...] = place(beta_c + cum_c + norm_k + norm_q, lane)
    scale = 1.0 / math.sqrt(T)
    ratio, solve, low = [], [], []
    for h in hs:
        r = jnp.where(
            lower, jnp.exp(jnp.where(lower, cum_c[h] - cum_row[h : h + 1], 0.0)), 0.0
        )
        ratio.append(r)
        ratio_ref[h] = r
        rk = jnp.where(strict, r * rk_ref[h], 0.0)
        rk_ref[h] = rk
        low.append(rk * beta_c[h])
    for h in hs:
        same = (row // 2) == (lane // 2)
        solve.append(jnp.where(same, -low[h], 0.0) + eye)
    size = 2
    while size < T:
        block = (row // (2 * size) == lane // (2 * size)) & (row // size != lane // size)
        parts = [split(s) for s in solve]
        corner = [split(jnp.where(block, low[h], 0.0)) for h in hs]
        inner = [split(mm(corner[h], parts[h], NN)) for h in hs]
        solve = [solve[h] - mm(parts[h], inner[h], NN) for h in hs]
        size *= 2
    for h in hs:
        inv_ref[h] = solve[h]
        grow_c, grow_row = jnp.exp(cum_c[h]), jnp.exp(cum_row[h : h + 1])
        end = last[h : h + 1]
        tail_c = jnp.exp(end - cum_c[h])
        bv = beta_row[h : h + 1]
        w = mm(split(solve[h] * bv), v[h], NN)
        y = mm(split(solve[h] * (bv * grow_row * norm_k_row[h : h + 1])), k[h], NN)
        w_out_ref[h] = w
        y_ref[h] = y
        p = ratio[h] * p_ref[h]
        p_ref[h] = p
        du = mm(split(p), g[h], TN)
        du_ref[h] = du
        out_scale = tail_c * norm_k[h]
        maps_ref[h, 0] = jnp.exp(end) * eye - mm(k[h], split(out_scale * y), TN)
        maps_ref[h, 1] = mm(k[h], split(out_scale * w), TN)
        own = mm(q[h], split((grow_c * norm_q[h] * scale) * g[h].astype(F32)), TN)
        maps_ref[h, 2] = own - mm(split(y), split(du), TN)


def group_kernel(maps_ref, out_ref):
    z = lax.axis_index("seq_0")
    phi = [split(maps_ref[x, 0]) for x in range(4)]
    off = [maps_ref[x, 1] for x in range(4)]
    loc = [maps_ref[x, 2] for x in range(4)]
    first = split(mm(phi[1], phi[0], NN))
    second = split(mm(phi[3], phi[2], NN))
    off_a = mm(phi[1], split(off[0]), NN) + off[1]
    off_b = mm(phi[3], split(off[2]), NN) + off[3]
    loc_a = mm(phi[0], split(loc[1]), TN) + loc[0]
    loc_b = mm(phi[2], split(loc[3]), TN) + loc[2]
    whole = mm(second, first, NN)
    later = mm(second, split(off_a), NN) + off_b
    earlier = mm(first, split(loc_b), TN) + loc_a
    for to in range(out_ref.shape[0]):
        out_ref[to, 0] = whole
        out_ref[to, 1] = jnp.where(to > z, later, earlier)


def spread_kernel(start_ref, end_ref, groups_ref, maps_ref, out_ref):
    z, x = lax.axis_index("seq_0"), lax.axis_index("seq_1")
    count = groups_ref.shape[0]
    state, grad = start_ref[x], end_ref[x]
    for step in range(count - 1):
        back = count - 1 - step
        ahead = mm(split(groups_ref[step, 0]), split(state), NN) + groups_ref[step, 1]
        behind = mm(split(groups_ref[back, 0]), split(grad), TN) + groups_ref[back, 1]
        state = jnp.where(step < z, ahead, state)
        grad = jnp.where(back > z, behind, grad)
    for step in range(4):
        back = 3 - step
        out_ref[step, 0] = state
        out_ref[back, 1] = grad
        if step < 3:
            state = mm(split(maps_ref[step, 0]), split(state), NN) + maps_ref[step, 1]
            grad = mm(split(maps_ref[back, 0]), split(grad), TN) + maps_ref[back, 2]


def finish_kernel(
    ends_ref, maps_ref, q_ref, k_ref, v_ref, g_ref, inv_ref, ratio_ref, rk_ref, p_ref, w_ref,
    y_ref, du_ref, rows_ref, cols_ref, x_hbm,
    dq_ref, dk_ref, dv_ref, bound_ref, logit_ref, term_ref, x_ref, sem,
):
    fetch = pltpu.make_async_copy(x_hbm, x_ref, sem)
    fetch.start()
    heads = maps_ref.shape[0]
    hs = range(heads)
    row, lane = ids((T, T))
    strict = row > lane
    scale = 1.0 / math.sqrt(T)
    cols, rows = cols_ref[...], rows_ref[...]
    decay_cols, beta_cols, decay_rows, ends = [], [], [], []
    for h in hs:
        span = slice(h * T, (h + 1) * T)
        q, k, g = q_ref[:, span], k_ref[:, span], g_ref[:, span]
        qf, kf, vf = q.astype(F32), k.astype(F32), v_ref[:, span].astype(F32)
        beta = cols[:, h : h + 1]
        cum = cols[:, heads + h : heads + h + 1]
        norm_k = cols[:, 2 * heads + h : 2 * heads + h + 1]
        norm_q = cols[:, 3 * heads + h : 3 * heads + h + 1]
        norm_k_row = rows[2 * heads + h : 2 * heads + h + 1]
        end = rows[heads + h : heads + h + 1, T - 1 : T]
        grow, tail = jnp.exp(cum), jnp.exp(end - cum)
        m0, d = ends_ref[h, 0], ends_ref[h, 1]
        m_parts, d_parts = split(m0), split(d)
        u = w_ref[h] - mm(split(y_ref[h]), m_parts, NN)
        du = du_ref[h] + (tail * norm_k) * mm(k, d_parts, NN)
        u_parts = split(u)
        db = mm(split(inv_ref[h]), split(du), TN)
        db_parts = split(db)
        bound_ref[0, h] = mm(split(maps_ref[h, 0]), d_parts, TN) + maps_ref[h, 2]
        km = norm_k * mm(k, m_parts, NN)
        z = vf - grow * km
        dv_ref[:, span] = beta * db
        kn = norm_k * kf
        qn = (norm_q * scale) * qf
        dkn = -(beta * grow) * mm(db_parts, m_parts, NT)
        da = jnp.where(strict, -mm(db_parts, u_parts, NT), 0.0)
        ratio = ratio_ref[h]
        rka = da * rk_ref[h]
        hm = beta * ratio * da
        dkn = dkn + mm(split((hm + hm.T) * norm_k_row), k, NN)
        dp = mm(g, u_parts, NT)
        ds = ratio * dp
        dqn = mm(split(ds * norm_k_row), k, NN)
        dkn = dkn + mm(split(ds * (norm_q * scale)), q, TN)
        dom = mm(g, m_parts, NT)
        dqn = dqn + grow * dom
        dkt = tail * mm(u_parts, d_parts, NT)
        dkn = dkn + dkt
        both = beta * rka + dp * p_ref[h]
        tails = dkt * kn
        decay_cols.append(
            jnp.sum(both + grow * (dom * qn - beta * (db * km)) - tails, axis=1, keepdims=True)
        )
        beta_cols.append(jnp.sum(db * z + rka, axis=1, keepdims=True))
        decay_rows.append(jnp.sum(both, axis=0, keepdims=True))
        last = jnp.sum(
            jnp.sum(jnp.exp(end) * (d * m0) + tails, axis=0, keepdims=True), axis=1, keepdims=True
        )
        ends.append(jnp.broadcast_to(last, (1, T)))
        dot_q = jnp.sum(qf * dqn, axis=1, keepdims=True)
        dot_k = jnp.sum(kf * dkn, axis=1, keepdims=True)
        dq_ref[:, span] = (norm_q * scale) * (dqn - qf * (norm_q * norm_q * dot_q))
        dk_ref[:, span] = norm_k * (dkn - kf * (norm_k * norm_k * dot_k))
    turned = place(decay_cols + beta_cols, lane).T
    lane_one = lane[:heads]
    dcum = turned[:heads] - jnp.concatenate(decay_rows, axis=0)
    dcum = dcum + jnp.where(lane_one == T - 1, jnp.concatenate(ends, axis=0), 0.0)
    lower_ones = jnp.where(row >= lane, 1.0, 0.0).astype(BF16)
    ddecay = mm(split3(dcum), lower_ones, NN)
    beta_row = rows[:heads]
    dbeta = turned[heads : 2 * heads] * beta_row * (1.0 - beta_row)
    dshift = ddecay * rows[5 * heads : 6 * heads]
    logit = jnp.concatenate([dbeta, dshift], axis=0)
    logit_ref[...] = logit
    rate_sum = jnp.sum(ddecay * rows[4 * heads : 5 * heads], axis=1, keepdims=True)
    bias_sum = jnp.sum(dshift, axis=1, keepdims=True)
    param = jnp.broadcast_to(jnp.concatenate([rate_sum, bias_sum], axis=0), (2 * heads, T))
    high, low = split(logit)
    fetch.wait()
    pieces = term_ref.shape[0]
    width = x_ref.shape[1] // pieces
    for s in range(pieces):
        x = x_ref[:, s * width : (s + 1) * width]
        term_ref[s, :, :width] = lax.dot_general(
            high, x, NN, preferred_element_type=F32
        ) + lax.dot_general(low, x, NN, preferred_element_type=F32)
        term_ref[s, :, width:] = param


def window_kernel(q_ref, g_ref, own_ref, near_ref, far_ref, dq_ref, stat_ref):
    kv_refs = (own_ref, near_ref, far_ref)
    z, x = lax.axis_index("seq_0"), lax.axis_index("seq_1")
    row, lane = ids((T, T))
    gap = row - lane
    scale = 1.0 / math.sqrt(T)
    q, g = q_ref[...], g_ref[...]
    scores = []
    tiles = [(a, b) for a in range(4) for b in range(3)]
    for a, b in tiles:
        spread = gap + (jnp.where(x >= a, a, a - 4) + 4 * b) * T
        ok = (spread >= 0) & (spread < jnp.where(z >= b, WINDOW, 0))
        s = lax.dot_general(q, kv_refs[b][a, 0], NT, preferred_element_type=F32) * scale
        scores.append(jnp.where(ok, s, -1e30))
    top = scores[0]
    for s in scores[1:]:
        top = jnp.maximum(top, s)
    top = jnp.max(top, axis=1, keepdims=True)
    weights = [jnp.exp(s - top) for s in scores]
    total = weights[0]
    for w in weights[1:]:
        total = total + w
    total = 1.0 / jnp.sum(total, axis=1, keepdims=True)
    weights = [w * total for w in weights]
    slopes, terms = [], None
    for (a, b), w in zip(tiles, weights):
        slope = lax.dot_general(g, kv_refs[b][a, 1], NT, preferred_element_type=F32)
        slopes.append(slope)
        terms = w * slope if terms is None else terms + w * slope
    terms = jnp.sum(terms, axis=1, keepdims=True)
    stat_ref[...] = place([top, total, terms], lane).T[:8]
    dq = None
    for (a, b), w, slope in zip(tiles, weights, slopes):
        part = mm(split(w * (slope - terms) * scale), kv_refs[b][a, 0], NN)
        dq = part if dq is None else dq + part
    dq_ref[...] = dq


def key_kernel(
    k_ref, v_ref, own_ref, near_ref, far_ref, own_stat, near_stat, far_stat, dk_ref, dv_ref
):
    qg_refs, stat_refs = (own_ref, near_ref, far_ref), (own_stat, near_stat, far_stat)
    z, x = lax.axis_index("seq_0"), lax.axis_index("seq_1")
    count = lax.axis_size("seq_0")
    row, lane = ids((T, T))
    gap = lane - row
    scale = 1.0 / math.sqrt(T)
    k, v = k_ref[...], v_ref[...]
    dk, dv = jnp.zeros((T, T), F32), jnp.zeros((T, T), F32)
    for b in range(3):
        for a in range(4):
            spread = gap + (jnp.where(x >= a, -a, 4 - a) + 4 * b) * T
            ok = (spread >= 0) & (spread < jnp.where(z + b < count, WINDOW, 0))
            q, g, stat = qg_refs[b][a, 0], qg_refs[b][a, 1], stat_refs[b][a]
            s = lax.dot_general(k, q, NT, preferred_element_type=F32) * scale
            w = jnp.exp(jnp.where(ok, s - stat[0:1], -1e30)) * stat[1:2]
            slope = lax.dot_general(v, g, NT, preferred_element_type=F32)
            dv = dv + mm(split(w), g, NN)
            dk = dk + mm(split(w * (slope - stat[2:3]) * scale), q, NN)
    dk_ref[...] = dk
    dv_ref[...] = dv


def input_kernel(near_ref, far_ref, own_ref, four_ref, two_ref, one_ref, out_ref, rows_ref, w_ref):
    half = near_ref.shape[0]
    rows_ref[:half, :] = near_ref[...]
    rows_ref[half:, :] = far_ref[...]
    places = (
        (0, own_ref, 0), (4, four_ref, 0), (2, two_ref, 0), (6, two_ref, 2),
        (1, one_ref, 0), (5, one_ref, 1), (3, one_ref, 2), (7, one_ref, 3),
    )
    for source, ref, at in places:
        w_ref[8 * source : 8 * source + 8, :] = ref[at].astype(F32)
    high, low = split(rows_ref[...])
    w = w_ref[...].astype(BF16)
    out_ref[...] = lax.dot_general(high, w, TN, preferred_element_type=F32) + lax.dot_general(
        low, w, TN, preferred_element_type=F32
    )


VM = pl.BlockSpec(memory_space=pltpu.VMEM)
SM = pl.BlockSpec(memory_space=pltpu.SMEM)
ANY = pl.BlockSpec(memory_space=pl.ANY)


def f32(*shape):
    return jax.ShapeDtypeStruct(shape, F32)


def call(kernel, outs, specs, *args, flops=10**8, scratch=(), limit=24 * 2**20):
    return run(kernel, outs, specs, args, flops, scratch, limit)


def exchange(value, axis):
    return lax.all_to_all(value, axis, split_axis=0, concat_axis=0, tiled=True)


def run(kernel, outs, specs, args, flops, scratch, limit):
    return pl.pallas_call(
        kernel,
        out_shape=outs,
        in_specs=specs,
        out_specs=jax.tree.map(lambda _: VM, outs),
        scratch_shapes=scratch,
        cost_estimate=pl.CostEstimate(flops=flops, bytes_accessed=4 * 10**6, transcendentals=0),
        compiler_params=pltpu.CompilerParams(vmem_limit_bytes=limit),
    )(*args)


WHOLE = 60 * 1024 * 1024


def up_by(value, by, count):
    pairs = [(i, i + by) for i in range(count) if 0 <= i + by < count]
    return lax.ppermute(value, "seq_0", pairs)


def turn(value, axis, by, count):
    return lax.ppermute(value, axis, [(i, (i + by) % count) for i in range(count)])


def swap(value, bit, count):
    return lax.ppermute(value, "head", [(i, i ^ bit) for i in range(count)])


def shards(
    layer_input, beta_weight, decay_weight, log_rate, decay_bias, delta_query, delta_key,
    delta_value, delta_out_grad, state_init, state_grad_next, attn_query, attn_key, attn_value,
    attn_out_grad,
):
    z_count, x_count = lax.axis_size("seq_0"), lax.axis_size("seq_1")
    head_count = lax.axis_size("head")
    heads = beta_weight.shape[0]
    width = layer_input.shape[1]
    pieces = z_count * x_count
    others = range(1, x_count)

    mine = jnp.stack([attn_key, attn_value, attn_query, attn_out_grad])
    line = [mine] + [turn(mine, "seq_1", d, x_count) for d in others]

    bf16_half = jax.ShapeDtypeStruct((4, 2 * heads, width // head_count), BF16)
    maps, inv, ratio, rk, p, w, y, du, rows, cols, *chunks = call(
        prepare_kernel,
        (f32(heads, 3, T, T),) + (f32(heads, T, T),) * 7 + (f32(6 * heads, T), f32(T, T))
        + (bf16_half,) * 2,
        [ANY, VM, VM, SM, SM, VM, VM, VM, VM],
        layer_input, beta_weight, decay_weight, log_rate, decay_bias, delta_query, delta_key,
        delta_value, delta_out_grad,
        scratch=[
            pltpu.VMEM((2 * heads, width), BF16), pltpu.VMEM((T, width), BF16),
            pltpu.SemaphoreType.DMA,
        ],
        limit=WHOLE,
    )
    blocks = exchange(maps, "seq_1")
    kv, qg = jnp.stack([a[:2] for a in line]), jnp.stack([a[2:] for a in line])
    kv_all = [kv] + [up_by(kv, d, z_count) for d in (1, 2)]
    qg_all = [qg] + [up_by(qg, -d, z_count) for d in (1, 2)]
    groups = call(group_kernel, f32(z_count, 2, T, T), [VM], blocks)

    groups = exchange(groups, "seq_0")
    dq_attn, stat = call(
        window_kernel,
        (f32(T, T), f32(8, T)),
        [VM] * 5,
        attn_query, attn_out_grad, *kv_all,
    )
    stat = jnp.stack([stat] + [turn(stat, "seq_1", d, x_count) for d in others])
    stat_all = [stat] + [up_by(stat, -d, z_count) for d in (1, 2)]
    dk_attn, dv_attn = call(
        key_kernel,
        (f32(T, T), f32(T, T)),
        [VM] * 8,
        attn_key, attn_value, *qg_all, *stat_all,
    )
    own = chunks[0]
    four = swap(chunks[1], 4, head_count)
    two = swap(jnp.concatenate([own[2:], four[2:]]), 2, head_count)
    one = swap(jnp.stack([own[1], four[1], two[1], two[3]]), 1, head_count)

    ends = call(
        spread_kernel,
        f32(x_count, 2, T, T),
        [VM] * 4,
        state_init, state_grad_next, groups, blocks,
    )
    ends = exchange(ends, "seq_1")

    dq, dk, dv, bound, logit, terms = call(
        finish_kernel,
        (f32(T, heads * T),) * 3
        + (f32(1, heads, T, T), f32(2 * heads, T), f32(pieces, 2 * heads, width // pieces + T)),
        [VM] * 15 + [ANY],
        ends, maps, delta_query, delta_key, delta_value, delta_out_grad, inv, ratio, rk, p, w, y,
        du, rows, cols, layer_input,
        scratch=[pltpu.VMEM((T, width), BF16), pltpu.SemaphoreType.DMA],
        limit=WHOLE,
    )
    terms = exchange(terms, SEQ)
    every = jnp.concatenate([logit, swap(logit, 1, head_count)])
    every = jnp.concatenate([every, swap(every, 2, head_count)])
    others = swap(every, 4, head_count)
    input_grad = call(
        input_kernel,
        f32(T, width // head_count),
        [VM] * 6,
        every, others, own, four, two, one,
        scratch=[
            pltpu.VMEM((2 * heads * head_count, T), F32),
            pltpu.VMEM((2 * heads * head_count, width // head_count), F32),
        ],
    )
    terms = jnp.sum(terms, axis=0)
    part = width // pieces
    return (
        dq, dk, dv, bound, input_grad,
        terms[:heads, :part], terms[heads:, :part],
        terms[:heads, part], terms[heads:, part],
        dq_attn, dk_attn, dv_attn,
    )


def solution(mesh):
    torus = Mesh(mesh.devices.reshape(8, 4, mesh.shape["head"]), ("seq_0", "seq_1", "head"))
    tokens, by_head = P(SEQ, "head"), P("head", None, None)
    in_specs = (
        P(SEQ, None), P("head", None), P("head", None), P("head"), P("head"),
        tokens, tokens, tokens, tokens, by_head, by_head, tokens, tokens, tokens, tokens,
    )
    out_specs = (
        tokens, tokens, tokens, P(SEQ, "head", None, None), tokens,
        P("head", SEQ), P("head", SEQ), P("head"), P("head"), tokens, tokens, tokens,
    )

    return jax.shard_map(
        shards, mesh=torus, in_specs=in_specs, out_specs=out_specs, check_vma=False
    )
```
